1024 devices in a mesh: dp: 2 (over z_hi), dom: 64 (over z_lo, y), tensor: 8 (over x, core).
Axes of the slice: x: 4, y: 4, z: 32 (z_hi: 2, z_lo: 16; z = z_hi * 16 + z_lo), core: 2. Of those that a mesh axis runs over, the one named last changes fastest.
Arguments:
- states: bfloat16 [2, 32768, 512], P('dp', 'dom'), may hold values from -60 to 60, as said below
- w_query: bfloat16 [512, 512], P(None, 'tensor'), as said below
- w_key: bfloat16 [512, 512], P(None, 'tensor'), as said below
- w_value: bfloat16 [512, 512], P(None, 'tensor'), may hold values from -0.25 to 0.25
- w_out: bfloat16 [512, 512], P('tensor'), may hold values from -0.25 to 0.25
- send_blocks: int32 [64, 4, 2], P('dom'), may hold values from 0 to 3
- neighbor_blocks: int32 [256, 3], P('dom'), may hold values from 0 to 11, as said below
- cotangent: bfloat16 [2, 32768, 512], P('dp', 'dom'), may hold values from -6 to 6
Outputs:
- update: bfloat16 [2, 32768, 512], P('dp', 'dom', 'tensor')
- branch_grad: bfloat16 [2, 32768, 512], P('dp', 'dom', 'tensor')
- grad_query: float32 [512, 512], P(None, 'tensor')
- grad_key: float32 [512, 512], P(None, 'tensor')
- grad_value: float32 [512, 512], P(None, 'tensor')
- grad_out: float32 [512, 512], P('tensor')
The draws below stay inside these ranges and needn't reach their ends.
Inputs may be any that keep to these rules, and one draw needn't show every extreme that they name: `neighbor_blocks`: entries index the pool of the row's own partition; every pool entry from 4 on is named by some row of that partition. `states`: real entries. `w_query`: real entries. `w_key`: real entries.
All inputs are finite; a program needn't handle non-finite values.
Results may differ from the reference program's by a relative error of at most 0.02.
The reference program's roundings to bfloat16 on the way count: a program that leaves them out, or rounds other values in their place, can miss the bound.
Values may be sent and summed in bfloat16 or wider, within the bound.
A program may use at most 32 MiB of HBM per device.

```python
import math
import jax
import jax.numpy as jnp
from jax import lax

D = 512
HEADS = 8
BLK = 128
NB = 3
HOPS = 2
SEND = 2
BLK_DEV = 4
NOFF = 4
POOL = 12
PARTS_SIZE = 64
BLOCKS = 256
NODES = 32768
REPL = 2
N_TENSOR = 8


def query_key_pair(key):
    base_draw = jax.random.normal(jax.random.fold_in(key, 11), (D, D), jnp.float32) / math.sqrt(D)
    other_draw = jax.random.normal(jax.random.fold_in(key, 12), (D, D), jnp.float32) / math.sqrt(D)
    return (2.0 * base_draw, other_draw)


def draw_w_query(key, part):
    return query_key_pair(key)[0].astype(jnp.bfloat16)


def draw_w_key(key, part):
    return query_key_pair(key)[1].astype(jnp.bfloat16)


def draw_states(key, part):
    drawn_draw = jnp.clip(jax.random.normal(jax.random.fold_in(key, 31), (REPL, NODES, D), jnp.float32), -4.0, 4.0)
    return drawn_draw.astype(jnp.bfloat16)


def neighbor_rows(key):
    received = POOL - BLK_DEV
    length = BLK_DEV * NB
    covered = jax.random.permutation(jax.random.fold_in(key, 1), received) + BLK_DEV
    spares = jax.random.randint(jax.random.fold_in(key, 2), (length - received,), 0, POOL)
    listed = jnp.concatenate([covered.astype(jnp.int32), spares.astype(jnp.int32)])
    return jax.random.permutation(jax.random.fold_in(key, 3), listed).reshape(BLK_DEV, NB)


def draw_neighbor_blocks(key, part):
    key_list = jax.random.split(jax.random.fold_in(key, 41), PARTS_SIZE)
    return jax.vmap(neighbor_rows)(key_list).reshape(BLOCKS, NB).astype(jnp.int32)


def touch_ends(entries, rng, low, largest):
    longest = entries.shape.index(max(entries.shape))
    spots = []
    for shift in (0, 1):
        where = [jax.random.randint(jax.random.fold_in(rng, axis), (), 0, length) for axis, length in enumerate(entries.shape)]
        where[longest] = (where[longest] + shift) % entries.shape[longest]
        spots.append(tuple(where))
    return entries.at[spots[0]].set(low).at[spots[1]].set(largest)


def steps_of(own_key, shape, cuts, low, high):
    gain = 1.0
    for axis_at, parts in cuts:
        heights = jax.random.uniform(jax.random.fold_in(jax.random.fold_in(own_key, 6), axis_at), (parts,), jnp.float32, low / len(cuts), high / len(cuts))
        gain = gain * jnp.repeat(jnp.exp(heights), shape[axis_at] // parts).reshape((-1,) + (1,) * (len(shape) - 1 - axis_at))
    return gain


def scatter_about(own_key, extent, width, bound, pieces=(), kind=jnp.bfloat16):
    loudness = steps_of(own_key, extent, pieces, -0.22, 0.18) if pieces else 1.0
    values = jax.random.normal(own_key, extent, jnp.float32) * width * loudness
    return jnp.minimum(jnp.maximum(values, -bound), bound).astype(kind)


def setup_inputs(seed: int = 0) -> dict:
    keys = jax.random.split(jax.random.key(seed), 9)
    states = draw_states(jax.random.fold_in(keys[8], 71), 0)
    w_query = draw_w_query(jax.random.fold_in(keys[8], 71), 0)
    w_key = draw_w_key(jax.random.fold_in(keys[8], 71), 0)
    w_value = scatter_about(keys[3], (D, D), D ** -0.5, 0.25, ((1, 8),))
    w_out = scatter_about(keys[4], (D, D), D ** -0.5, 0.25, ((0, 8),))
    send_blocks = touch_ends(jax.random.randint(keys[5], (PARTS_SIZE, NOFF, SEND), 0, BLK_DEV), jax.random.fold_in(keys[5], 1), 0, BLK_DEV - 1).astype(jnp.int32)
    neighbor_blocks = draw_neighbor_blocks(jax.random.fold_in(keys[8], 71), 0)
    cotangent = scatter_about(keys[7], (REPL, NODES, D), 1.0, 6.0, ((0, 2), (1, 64)))
    return dict(states=states, w_query=w_query, w_key=w_key, w_value=w_value, w_out=w_out, send_blocks=send_blocks, neighbor_blocks=neighbor_blocks, cotangent=cotangent)


def offset_list(hops):
    result = []
    for section in range(1, hops + 1):
        result.append(section)
        result.append(-section)
    return result

def normalize(states):
    values = states.astype(jnp.float32)
    inverse = lax.rsqrt(lax.optimization_barrier(jnp.mean(values * values, axis=-1, keepdims=True)) + 1e-05)
    return (values * inverse, inverse)

def product(form, left, right):
    return jnp.einsum(form, left.astype(jnp.float32), right.astype(jnp.float32))

def rounded(values):
    return lax.optimization_barrier(values.astype(jnp.bfloat16)).astype(jnp.float32)

def attend(queries, key_pool, key_index, grad_heads, head_count):
    replicas, blocks, block_rows, widths = queries.shape
    head_size = widths // head_count
    shrink = 1.0 / math.sqrt(head_size)
    listed = key_index.shape[1]
    chosen = jnp.take(key_pool, key_index.reshape(-1), axis=1)
    chosen = chosen.reshape(replicas, blocks, listed * block_rows, 2, head_count, head_size)
    key_rows = chosen[:, :, :, 0]
    value_rows = chosen[:, :, :, 1]
    query_heads = queries.reshape(replicas, blocks, block_rows, head_count, head_size)
    grad_split = grad_heads.reshape(replicas, blocks, block_rows, head_count, head_size)
    scores = product('rbqhe,rbkhe->rbhqk', query_heads, key_rows) * shrink
    highest = lax.optimization_barrier(jnp.max(scores, axis=-1, keepdims=True))
    powers = jnp.exp(scores - highest)
    weights = powers / lax.optimization_barrier(jnp.sum(powers, axis=-1, keepdims=True))
    weights_low = weights.astype(jnp.bfloat16)
    mixed_rows = product('rbhqk,rbkhe->rbqhe', weights_low, value_rows).astype(jnp.bfloat16)
    prob_grad = product('rbqhe,rbkhe->rbhqk', grad_split, value_rows)
    score_grad = weights * (prob_grad - lax.optimization_barrier(jnp.sum(weights * prob_grad, axis=-1, keepdims=True)))
    score_low = (score_grad * shrink).astype(jnp.bfloat16)
    query_grad = product('rbhqk,rbkhe->rbqhe', score_low, key_rows).astype(jnp.bfloat16)
    key_grad = product('rbhqk,rbqhe->rbkhe', score_low, query_heads)
    value_grad = product('rbhqk,rbqhe->rbkhe', weights_low, grad_split)
    chosen_grad = jnp.stack([key_grad, value_grad], axis=3).reshape(replicas, blocks, listed, block_rows, 2 * widths)
    pool_size = key_pool.shape[1]
    chooser = (key_index[:, :, None] == jnp.arange(pool_size, dtype=jnp.int32)[None, None, :]).astype(jnp.float32)
    pool_grad = jnp.einsum('bnp,rbnqc->rpqc', chooser, chosen_grad, precision=lax.Precision.HIGHEST)
    return (mixed_rows.reshape(replicas, blocks, block_rows, widths), query_grad.reshape(replicas, blocks, block_rows, widths), pool_grad)

def reference(states, w_query, w_key, w_value, w_out, send_blocks, neighbor_blocks, cotangent):
    normed, inverse = normalize(states)
    unit_rows = normed.astype(jnp.bfloat16)
    flat_unit = unit_rows.reshape(-1, D)
    queries = jnp.dot(flat_unit, w_query, preferred_element_type=jnp.float32).astype(jnp.bfloat16)
    queries = queries.reshape(REPL, PARTS_SIZE, BLK_DEV, BLK, D)
    paired = jnp.dot(flat_unit, jnp.concatenate([w_key, w_value], axis=1), preferred_element_type=jnp.float32).astype(jnp.bfloat16)
    paired = paired.reshape(REPL, PARTS_SIZE, BLK_DEV, BLK, 2 * D)
    flat_cot = cotangent.reshape(-1, D)
    grad_heads = jnp.dot(flat_cot, w_out.T, preferred_element_type=jnp.float32).astype(jnp.bfloat16)
    grad_heads = grad_heads.reshape(REPL, PARTS_SIZE, BLK_DEV, BLK, D)
    offsets = offset_list(HOPS)

    def one_part(part):
        part = part.astype(jnp.int32)
        gathered = [paired[:, part]]
        for slot_group, distance in enumerate(offsets):
            source = (part - distance) % PARTS_SIZE
            picked = send_blocks[source, slot_group]
            gathered.append(jnp.take(paired[:, source], picked, axis=1))
        key_pool = jnp.concatenate(gathered, axis=1)
        near_list = lax.dynamic_slice_in_dim(neighbor_blocks, part * BLK_DEV, BLK_DEV, 0)
        key_index = jnp.concatenate([jnp.arange(BLK_DEV, dtype=jnp.int32)[:, None], near_list], axis=1)
        mixed_rows, query_grad, pool_grad = attend(queries[:, part], key_pool, key_index, grad_heads[:, part], HEADS)
        return (mixed_rows, query_grad, pool_grad[:, :BLK_DEV], pool_grad[:, BLK_DEV:].astype(jnp.bfloat16))
    mixed_rows, query_grad, own_grad, remote = lax.map(one_part, jnp.arange(PARTS_SIZE, dtype=jnp.int32))
    summed = jnp.transpose(own_grad, (0, 2, 1, 3, 4))
    remote = jnp.transpose(lax.optimization_barrier(remote), (0, 2, 1, 3, 4)).astype(jnp.float32)
    parts_all = jnp.arange(PARTS_SIZE, dtype=jnp.int32)
    for slot_group, distance in enumerate(offsets):
        owners = (parts_all - distance) % PARTS_SIZE
        picked = send_blocks[owners, slot_group]
        summed = summed.at[owners[:, None], picked].add(remote[:, slot_group * SEND:(slot_group + 1) * SEND])
    pair_grad = jnp.transpose(summed, (2, 0, 1, 3, 4)).astype(jnp.bfloat16).reshape(-1, 2 * D)
    key_grad = pair_grad[:, :D]
    value_grad = pair_grad[:, D:]
    flat_mixed = jnp.transpose(mixed_rows, (1, 0, 2, 3, 4)).reshape(-1, D)
    flat_query_grad = jnp.transpose(query_grad, (1, 0, 2, 3, 4)).reshape(-1, D)
    slab_width = D // N_TENSOR
    update_sum = jnp.zeros((flat_unit.shape[0], D), jnp.float32)
    unit_sum = jnp.zeros((flat_unit.shape[0], D), jnp.float32)
    for group in range(N_TENSOR):
        columns = slice(group * slab_width, (group + 1) * slab_width)
        update_sum = update_sum + rounded(jnp.dot(flat_mixed[:, columns], w_out[columns], preferred_element_type=jnp.float32))
        unit_term = jnp.dot(flat_query_grad[:, columns], w_query[:, columns].T, preferred_element_type=jnp.float32)
        unit_term = unit_term + jnp.dot(key_grad[:, columns], w_key[:, columns].T, preferred_element_type=jnp.float32)
        unit_term = unit_term + jnp.dot(value_grad[:, columns], w_value[:, columns].T, preferred_element_type=jnp.float32)
        unit_sum = unit_sum + rounded(unit_term)
    update = update_sum.astype(jnp.bfloat16).reshape(REPL, NODES, D)
    flat_normed = normed.reshape(-1, D)
    row_mean = lax.optimization_barrier(jnp.mean(unit_sum * flat_normed, axis=-1, keepdims=True))
    branch_grad = (inverse.reshape(-1, 1) * (unit_sum - flat_normed * row_mean)).astype(jnp.bfloat16)
    branch_grad = branch_grad.reshape(REPL, NODES, D)
    factor = 1.0 / math.sqrt(REPL * NODES)
    grad_query = jnp.dot(flat_unit.T, flat_query_grad, preferred_element_type=jnp.float32) * factor
    grad_key = jnp.dot(flat_unit.T, key_grad, preferred_element_type=jnp.float32) * factor
    grad_value = jnp.dot(flat_unit.T, value_grad, preferred_element_type=jnp.float32) * factor
    grad_out = jnp.dot(flat_mixed.T, flat_cot, preferred_element_type=jnp.float32) * factor
    return (update, branch_grad, grad_query, grad_key, grad_value, grad_out)
```

```python
import functools
import math

import jax
import jax.numpy as jnp
from jax import lax
from jax.experimental import pallas as pl
from jax.experimental.pallas import tpu as pltpu
from jax.sharding import PartitionSpec as P

BLK = 128
HD = 64
D = 512
NBLK = 4
ROWS = NBLK * BLK
OFFSETS = (1, -1, 2, -2)
NY = 4
F32 = jnp.float32
BF16 = jnp.bfloat16
MESH = pl.DeviceIdType.MESH
EXP_SCALE = (1.0 / math.sqrt(HD)) / math.log(2.0)
SHRINK = 1.0 / math.sqrt(HD)


def nn(a, b):
    return lax.dot_general(a, b, (((1,), (0,)), ((), ())), preferred_element_type=F32)


def nt(a, b):
    return lax.dot_general(a, b, (((1,), (1,)), ((), ())), preferred_element_type=F32)


class Sizes:
    def __init__(self, dp, dom, t):
        self.DP, self.DOM, self.T = dp, dom, t
        nz = dom // NY
        self.ZR = min(4, nz)
        self.ZQ = nz // self.ZR
        self.NA = NY * self.ZR
        self.NB = self.ZQ * dp
        self.CR = 512 // self.NA
        self.BR = self.CR // self.NB
        self.SLAB = D // t
        self.factor = 1.0 / math.sqrt(dp * dom * ROWS)


def kernel(
    g,
    sb, nb, x_ref, wq_ref, wk_ref, wv_ref, wo_ref, cot_ref,
    upd_ref, br_ref, gq_ref, gk_ref, gv_ref, go_ref,
    unit, unit_t, x_t, wall, wo_t, wo_pad, inv_row, bm, kv_own, pool, pool_t, kvs,
    cg, mix_t, qg_t, xx, own, ret_s, ret_r,
    us, ur, ts, tr, rd_s, rd_r, gq_t,
    pay1, rsa1, tmp1, rsb_s1, rsb_r1, agb1, aga1,
    pay2, rsa2, tmp2, rsb_s2, rsb_r2, agb2, aga2,
    kv_ss, kv_rs, ret_ss, ret_rs, u_ss, u_rs, t_ss, t_rs, d_ss, d_rs,
    a1_ss, a1_rs, b1_ss, b1_rs, gb1_ss, gb1_rs, ga1_ss, ga1_rs,
    a2_ss, a2_rs, b2_ss, b2_rs, gb2_ss, gb2_rs, ga2_ss, ga2_rs,
):
    dp = lax.axis_index("dp")
    dom = lax.axis_index("dom")
    tn = lax.axis_index("tensor")
    y = lax.rem(dom, NY)
    z = dom // NY
    zr = lax.rem(z, g.ZR)
    zq = z // g.ZR
    my_a = y * g.ZR + zr
    my_b = dp * g.ZQ + zq

    def dom_peer(o):
        return (dp, lax.rem(dom + (o + g.DOM), g.DOM), tn)

    def t_index(k):
        return lax.rem(tn + k, g.T)

    def t_peer(k):
        return (dp, dom, t_index(k))

    a_offs = [(dy, dz) for dy in range(NY) for dz in range(g.ZR)][1:]
    b_offs = [(dd, dq) for dd in range(g.DP) for dq in range(g.ZQ)][1:]

    def a_peer(off):
        y2 = lax.rem(y + off[0], NY)
        r2 = lax.rem(zr + off[1], g.ZR)
        return y2 * g.ZR + r2, (dp, (zq * g.ZR + r2) * NY + y2, tn)

    def b_peer(off):
        d2 = lax.rem(dp + off[0], g.DP)
        q2 = lax.rem(zq + off[1], g.ZQ)
        return d2 * g.ZQ + q2, (d2, (q2 * g.ZR + zr) * NY + y, tn)

    peers = [dom_peer(o) for o in OFFSETS]
    peers += [t_peer(k) for k in range(1, g.T)]
    peers += [a_peer(off)[1] for off in a_offs]
    peers += [b_peer(off)[1] for off in b_offs]
    barrier = pltpu.get_barrier_semaphore()
    for peer in peers:
        pl.semaphore_signal(barrier, inc=1, device_id=peer, device_id_type=MESH)

    def remote(src, dst, ss, rs, peer):
        copy = pltpu.make_async_remote_copy(
            src_ref=src, dst_ref=dst, send_sem=ss, recv_sem=rs, device_id=peer, device_id_type=MESH
        )
        copy.start()
        return copy

    started = []

    wall[...] = jnp.concatenate(
        [wk_ref[...], wv_ref[...], wq_ref[...], jnp.zeros((D, HD), BF16)], axis=1
    )
    for b in range(NBLK):
        rows = slice(b * BLK, (b + 1) * BLK)
        xf = x_ref[rows, :].astype(F32)
        inv = lax.rsqrt(jnp.mean(xf * xf, axis=-1, keepdims=True) + 1e-05)
        unit[rows, :] = (xf * inv).astype(BF16)
    for b in range(NBLK):
        rows = slice(b * BLK, (b + 1) * BLK)
        block = nn(unit[rows, :], wall[:, : 2 * HD]).astype(BF16)
        kv_own[b] = block
        pool[b] = block
    for i in range(4):
        for c in range(2):
            kvs[i, c] = kv_own[sb[0, i, c]]
    pl.semaphore_wait(barrier, len(peers))
    kv_copies = []
    for i in (2, 3, 0, 1):
        kv_copies.append(
            remote(kvs.at[i], pool.at[pl.ds(NBLK + 2 * i, 2)], kv_ss.at[i], kv_rs.at[i], dom_peer(OFFSETS[i]))
        )

    wo_pad[0:HD, :] = jnp.zeros((HD, D), BF16)
    wo_pad[HD : 2 * HD, :] = wo_ref[...]
    for b in range(NBLK):
        rows = slice(b * BLK, (b + 1) * BLK)
        bm[b, 0:BLK, :] = nn(unit[rows, :], wall[:, 2 * HD :]).astype(BF16)
        bm[b, BLK : 2 * BLK, :] = nt(cot_ref[rows, :], wo_pad[...]).astype(BF16)
        pool_t[b] = kv_own[b].T
    for f in range(D // BLK):
        cols = slice(f * BLK, (f + 1) * BLK)
        for b in range(NBLK):
            x_t[cols, b * BLK : (b + 1) * BLK] = x_ref[b * BLK : (b + 1) * BLK, cols].T
        wo_t[cols, :] = wo_ref[:, cols].T
    square = jnp.zeros((1, ROWS), F32)
    for f in range(D // BLK):
        part = x_t[f * BLK : (f + 1) * BLK, :].astype(F32)
        square = square + jnp.sum(part * part, axis=0, keepdims=True)
    inv_lane = lax.rsqrt(square * (1.0 / D) + 1e-05)
    inv_row[...] = inv_lane
    for f in range(D // BLK):
        cols = slice(f * BLK, (f + 1) * BLK)
        unit_t[cols, :] = (x_t[cols, :].astype(F32) * inv_lane).astype(BF16)

    for copy in kv_copies:
        copy.wait_recv()
    for p in range(NBLK, 3 * NBLK):
        pool_t[p] = pool[p].T

    for b in range(NBLK):
        lists = [nb[b, n] for n in range(3)]
        kv_sel = jnp.concatenate([pool[b]] + [pool[i] for i in lists], axis=0)
        kv_sel_t = jnp.concatenate([pool_t[b]] + [pool_t[i] for i in lists], axis=1)
        both = nt(kv_sel, bm[b])
        scores = both[:, :BLK]
        prob_grad = both[:, BLK:]
        powers = jnp.exp2((scores - jnp.max(scores, axis=0, keepdims=True)) * EXP_SCALE)
        weights = powers * (1.0 / jnp.sum(powers, axis=0, keepdims=True))
        inner = jnp.sum(weights * prob_grad, axis=0, keepdims=True)
        score_low = (weights * (prob_grad - inner) * SHRINK).astype(BF16)
        pair = jnp.concatenate([score_low, weights.astype(BF16)], axis=1)
        grads = nn(pair, bm[b])
        for n in range(4):
            cg[4 * b + n] = grads[n * BLK : (n + 1) * BLK, :]
        outs = nn(kv_sel_t, pair)
        cols = slice(b * BLK, (b + 1) * BLK)
        qg_t[:, cols] = outs[0:HD, 0:BLK].astype(BF16)
        mix_t[:, cols] = outs[HD : 2 * HD, BLK : 2 * BLK].astype(BF16)

    def listed_sum(p, start):
        total = start
        for b in range(NBLK):
            for n in range(3):
                term = jnp.where(nb[b, n] == p, cg[4 * b + n + 1], 0.0)
                total = term if total is None else total + term
        return total

    ret_copies = []
    for i in (2, 3, 0, 1):
        for c in range(2):
            ret_s[i, c] = listed_sum(NBLK + 2 * i + c, None).astype(BF16)
        ret_copies.append(
            remote(ret_s.at[i], ret_r.at[i], ret_ss.at[i], ret_rs.at[i], dom_peer(-OFFSETS[i]))
        )

    for k in range(g.T):
        us[k] = nn(wo_t[k * g.SLAB : (k + 1) * g.SLAB, :], mix_t[...]).astype(BF16)
    u_copies = []
    for k in range(1, g.T):
        u_copies.append(
            remote(us.at[t_index(k)], ur.at[k - 1], u_ss.at[k - 1], u_rs.at[k - 1], t_peer(k))
        )

    def scatter_a(pay, rsa, ss, rs):
        copies = []
        for k, off in enumerate(a_offs):
            index, peer = a_peer(off)
            copies.append(remote(pay.at[index], rsa.at[k], ss.at[k], rs.at[k], peer))
        return copies

    def scatter_b(copies, pay, rsa, tmp, rsb_s, rsb_r, ss, rs):
        total = pay[my_a].astype(F32)
        for k, copy in enumerate(copies):
            copy.wait_recv()
            total = total + rsa[k].astype(F32)
        tmp[...] = total
        for j in range(g.NB):
            rsb_s[j] = tmp[j * g.BR : (j + 1) * g.BR, :]
        copies = []
        for k, off in enumerate(b_offs):
            index, peer = b_peer(off)
            copies.append(remote(rsb_s.at[index], rsb_r.at[k], ss.at[k], rs.at[k], peer))
        return copies

    def gather_b(copies, rsb_s, rsb_r, agb, ss, rs):
        total = rsb_s[my_b]
        for k, copy in enumerate(copies):
            copy.wait_recv()
            total = total + rsb_r[k]
        agb[my_b] = total
        copies = []
        for k, off in enumerate(b_offs):
            copies.append(remote(agb.at[my_b], agb.at[my_b], ss.at[k], rs.at[k], b_peer(off)[1]))
        return copies

    def gather_a(copies, agb, tmp, aga, ss, rs):
        for copy in copies:
            copy.wait_recv()
        for j in range(g.NB):
            tmp[j * g.BR : (j + 1) * g.BR, :] = agb[j]
        aga[my_a] = tmp[...].astype(BF16)
        copies = []
        for k, off in enumerate(a_offs):
            copies.append(remote(aga.at[my_a], aga.at[my_a], ss.at[k], rs.at[k], a_peer(off)[1]))
        return copies

    grad_q = nn(qg_t[...], unit[...])
    grad_o = nn(mix_t[...], cot_ref[...])
    lane_blocks = D // BLK
    for a in range(g.NA):
        r, c = a // lane_blocks, a % lane_blocks
        row = r * g.CR
        cols = slice(c * BLK, (c + 1) * BLK)
        if row < HD:
            pay1[a] = grad_q[row : row + g.CR, cols].astype(BF16)
        else:
            pay1[a] = grad_o[row - HD : row - HD + g.CR, cols].astype(BF16)
    a1 = scatter_a(pay1, rsa1, a1_ss, a1_rs)
    started += a1

    for j in range(NBLK):
        own[j] = listed_sum(j, cg[4 * j])
    for b in range(NBLK):
        rows = slice(b * BLK, (b + 1) * BLK)
        query_grad = qg_t[:, rows].astype(F32).T.astype(BF16)
        xx[rows, 2 * HD :] = jnp.concatenate([query_grad, jnp.zeros((BLK, HD), BF16)], axis=1)

    b1 = scatter_b(a1, pay1, rsa1, tmp1, rsb_s1, rsb_r1, b1_ss, b1_rs)
    started += b1

    for copy in ret_copies:
        copy.wait_recv()
    for j in range(NBLK):
        total = own[j]
        for i in range(4):
            for c in range(2):
                total = total + jnp.where(sb[0, i, c] == j, ret_r[i, c].astype(F32), 0.0)
        xx[j * BLK : (j + 1) * BLK, : 2 * HD] = total.astype(BF16)

    for a in range(g.NA):
        rows = slice(a * g.CR, (a + 1) * g.CR)
        pay2[a] = nn(unit_t[rows, :], xx[:, : 2 * HD]).astype(BF16)
    a2 = scatter_a(pay2, rsa2, a2_ss, a2_rs)
    started += a2

    for k in range(g.T):
        rows = slice(k * g.SLAB, (k + 1) * g.SLAB)
        ts[k] = nt(wall[rows, :], xx[...]).astype(BF16)
    t_copies = []
    for k in range(1, g.T):
        t_copies.append(
            remote(ts.at[t_index(k)], tr.at[k - 1], t_ss.at[k - 1], t_rs.at[k - 1], t_peer(k))
        )
    dots = jnp.zeros((1, ROWS), F32)
    for k in range(g.T):
        rows = slice(k * g.SLAB, (k + 1) * g.SLAB)
        dots = dots + jnp.sum(ts[k].astype(F32) * x_t[rows, :].astype(F32), axis=0, keepdims=True)
    rd_s[...] = dots
    d_copies = []
    for k in range(1, g.T):
        d_copies.append(remote(rd_s, rd_r.at[k - 1], d_ss.at[k - 1], d_rs.at[k - 1], t_peer(k)))

    gb1 = gather_b(b1, rsb_s1, rsb_r1, agb1, gb1_ss, gb1_rs)
    b2 = scatter_b(a2, pay2, rsa2, tmp2, rsb_s2, rsb_r2, b2_ss, b2_rs)
    ga1 = gather_a(gb1, agb1, tmp1, aga1, ga1_ss, ga1_rs)

    total = us[tn].astype(F32)
    for k, copy in enumerate(u_copies):
        copy.wait_recv()
        total = total + ur[k].astype(F32)
    upd_ref[0] = total.T.astype(BF16)

    gb2 = gather_b(b2, rsb_s2, rsb_r2, agb2, gb2_ss, gb2_rs)

    total = ts[tn].astype(F32)
    for k, copy in enumerate(t_copies):
        copy.wait_recv()
        total = total + tr[k].astype(F32)
    for k, copy in enumerate(d_copies):
        copy.wait_recv()
        dots = dots + rd_r[k]
    inv_lane = inv_row[...]
    slab = x_t[pl.ds(pl.multiple_of(tn * g.SLAB, g.SLAB), g.SLAB), :].astype(F32) * inv_lane
    row_mean = dots * inv_lane * (1.0 / D)
    br_ref[0] = (inv_lane * (total - slab * row_mean)).T.astype(BF16)

    ga2 = gather_a(gb2, agb2, tmp2, aga2, ga2_ss, ga2_rs)

    for copy in ga1:
        copy.wait_recv()
    for a in range(g.NA):
        r, c = a // lane_blocks, a % lane_blocks
        row = r * g.CR
        cols = slice(c * BLK, (c + 1) * BLK)
        chunk = aga1[a].astype(F32) * g.factor
        if row < HD:
            gq_t[row : row + g.CR, cols] = chunk
        else:
            go_ref[row - HD : row - HD + g.CR, cols] = chunk
    for c in range(lane_blocks):
        cols = slice(c * BLK, (c + 1) * BLK)
        gq_ref[cols, :] = gq_t[:, cols].T
    for copy in ga2:
        copy.wait_recv()
    for a in range(g.NA):
        rows = slice(a * g.CR, (a + 1) * g.CR)
        chunk = aga2[a].astype(F32) * g.factor
        gk_ref[rows, :] = chunk[:, :HD]
        gv_ref[rows, :] = chunk[:, HD:]

    started += kv_copies + ret_copies + u_copies + t_copies + d_copies
    started += gb1 + b2 + ga1 + gb2 + ga2
    for copy in started:
        copy.wait_send()


def body(g, states, w_query, w_key, w_value, w_out, send_blocks, neighbor_blocks, cotangent):
    vmem = pl.BlockSpec(memory_space=pltpu.VMEM)
    smem = pl.BlockSpec(memory_space=pltpu.SMEM)
    sem = pltpu.SemaphoreType.DMA
    blocks = (BLK, 2 * HD)
    reduce_bufs = [
        pltpu.VMEM((g.NA, g.CR, 128), BF16),
        pltpu.VMEM((max(g.NA - 1, 1), g.CR, 128), BF16),
        pltpu.VMEM((g.CR, 128), F32),
        pltpu.VMEM((g.NB, g.BR, 128), F32),
        pltpu.VMEM((max(g.NB - 1, 1), g.BR, 128), F32),
        pltpu.VMEM((g.NB, g.BR, 128), F32),
        pltpu.VMEM((g.NA, g.CR, 128), BF16),
    ]
    na, nbb, nt_ = max(g.NA - 1, 1), max(g.NB - 1, 1), max(g.T - 1, 1)
    reduce_sems = [sem((n,)) for n in (na, na, nbb, nbb, nbb, nbb, na, na)]
    out = pl.pallas_call(
        functools.partial(kernel, g),
        out_shape=[
            jax.ShapeDtypeStruct((1, ROWS, g.SLAB), BF16),
            jax.ShapeDtypeStruct((1, ROWS, g.SLAB), BF16),
            jax.ShapeDtypeStruct((D, HD), F32),
            jax.ShapeDtypeStruct((D, HD), F32),
            jax.ShapeDtypeStruct((D, HD), F32),
            jax.ShapeDtypeStruct((HD, D), F32),
        ],
        in_specs=[smem, smem] + [vmem] * 6,
        out_specs=[vmem] * 6,
        scratch_shapes=[
            pltpu.VMEM((ROWS, D), BF16),
            pltpu.VMEM((D, ROWS), BF16),
            pltpu.VMEM((D, ROWS), BF16),
            pltpu.VMEM((D, 4 * HD), BF16),
            pltpu.VMEM((D, HD), BF16),
            pltpu.VMEM((2 * HD, D), BF16),
            pltpu.VMEM((1, ROWS), F32),
            pltpu.VMEM((NBLK, 2 * BLK, 2 * HD), BF16),
            pltpu.VMEM((NBLK,) + blocks, BF16),
            pltpu.VMEM((3 * NBLK,) + blocks, BF16),
            pltpu.VMEM((3 * NBLK,) + blocks, BF16),
            pltpu.VMEM((4, 2) + blocks, BF16),
            pltpu.VMEM((4 * NBLK,) + blocks, F32),
            pltpu.VMEM((HD, ROWS), BF16),
            pltpu.VMEM((HD, ROWS), BF16),
            pltpu.VMEM((ROWS, 4 * HD), BF16),
            pltpu.VMEM((NBLK,) + blocks, F32),
            pltpu.VMEM((4, 2) + blocks, BF16),
            pltpu.VMEM((4, 2) + blocks, BF16),
            pltpu.VMEM((g.T, g.SLAB, ROWS), BF16),
            pltpu.VMEM((nt_, g.SLAB, ROWS), BF16),
            pltpu.VMEM((g.T, g.SLAB, ROWS), BF16),
            pltpu.VMEM((nt_, g.SLAB, ROWS), BF16),
            pltpu.VMEM((1, ROWS), F32),
            pltpu.VMEM((nt_, 1, ROWS), F32),
            pltpu.VMEM((HD, D), F32),
        ]
        + reduce_bufs
        + reduce_bufs
        + [sem((4,))] * 4
        + [sem((nt_,))] * 6
        + reduce_sems
        + reduce_sems,
        compiler_params=pltpu.CompilerParams(
            collective_id=0, has_side_effects=True, vmem_limit_bytes=40 * 1024 * 1024
        ),
        name="layer",
    )(
        send_blocks, neighbor_blocks, states[0], w_query, w_key, w_value, w_out, cotangent[0]
    )
    return tuple(out)


def solution(mesh):
    placed = (
        P("dp", "dom", None),
        P(None, "tensor"),
        P(None, "tensor"),
        P(None, "tensor"),
        P("tensor", None),
        P("dom", None, None),
        P("dom", None),
        P("dp", "dom", None),
    )
    g = Sizes(mesh.shape["dp"], mesh.shape["dom"], mesh.shape["tensor"])
    return jax.shard_map(
        functools.partial(body, g),
        mesh=mesh,
        in_specs=placed,
        out_specs=(
            P("dp", "dom", "tensor"),
            P("dp", "dom", "tensor"),
            P(None, "tensor"),
            P(None, "tensor"),
            P(None, "tensor"),
            P("tensor", None),
        ),
        check_vma=False,
    )
```

```python
import functools
import math

import jax
import jax.numpy as jnp
from jax import lax
from jax.experimental import pallas as pl
from jax.experimental.pallas import tpu as pltpu
from jax.sharding import PartitionSpec as P

BLK = 128
HD = 64
D = 512
NBLK = 4
ROWS = NBLK * BLK
OFFSETS = (1, -1, 2, -2)
NY = 4
F32 = jnp.float32
BF16 = jnp.bfloat16
MESH = pl.DeviceIdType.MESH
EXP_SCALE = (1.0 / math.sqrt(HD)) / math.log(2.0)
SHRINK = 1.0 / math.sqrt(HD)


def nn(a, b):
    return lax.dot_general(a, b, (((1,), (0,)), ((), ())), preferred_element_type=F32)


def nt(a, b):
    return lax.dot_general(a, b, (((1,), (1,)), ((), ())), preferred_element_type=F32)


class Sizes:
    def __init__(self, dp, dom, t):
        self.DP, self.DOM, self.T = dp, dom, t
        nz = dom // NY
        self.ZR = min(4, nz)
        self.ZQ = nz // self.ZR
        self.NA = NY * self.ZR
        self.NB = self.ZQ * dp
        self.CR = 512 // self.NA
        self.SLAB = D // t
        self.factor = 1.0 / math.sqrt(dp * dom * ROWS)


def kernel(
    g,
    sb, nb, x_any, wq_any, wk_any, wv_any, wo_any, cot_any,
    upd_ref, br_ref, w_ref,
    x_ref, cot_ref, in_sems, unit, x_t, wall_t, wall, wo_t, wo_pad, inv_row, bm, kv_own, pool, pool_t, kvs,
    cg, mix_t, qg_t, xx, own, ret_s, ret_r,
    us, ur, ts, tr, rd_s, rd_r, kvg_t,
    pay1, rsa1, bb1, aga1, pay2, rsa2, bb2, aga2,
    kv_ss, kv_rs, ret_ss, ret_rs, u_ss, u_rs, t_ss, t_rs, d_ss, d_rs,
    a1_ss, a1_rs, b1_ss, b1_rs, ga1_ss, ga1_rs,
    a2_ss, a2_rs, b2_ss, b2_rs, ga2_ss, ga2_rs,
):
    dp = lax.axis_index("dp")
    dom = lax.axis_index("dom")
    tn = lax.axis_index("tensor")
    y = lax.rem(dom, NY)
    z = dom // NY
    zr = lax.rem(z, g.ZR)
    zq = z // g.ZR
    my_a = y * g.ZR + zr
    my_b = dp * g.ZQ + zq

    def dom_peer(o):
        return (dp, lax.rem(dom + (o + g.DOM), g.DOM), tn)

    def t_index(k):
        return lax.rem(tn + k, g.T)

    def t_peer(k):
        return (dp, dom, t_index(k))

    a_offs = [(dy, dz) for dy in range(NY) for dz in range(g.ZR)][1:]
    b_offs = [(dd, dq) for dd in range(g.DP) for dq in range(g.ZQ)][1:]

    def a_peer(off):
        y2 = lax.rem(y + off[0], NY)
        r2 = lax.rem(zr + off[1], g.ZR)
        return y2 * g.ZR + r2, (dp, (zq * g.ZR + r2) * NY + y2, tn)

    def b_peer(off):
        d2 = lax.rem(dp + off[0], g.DP)
        q2 = lax.rem(zq + off[1], g.ZQ)
        return d2 * g.ZQ + q2, (d2, (q2 * g.ZR + zr) * NY + y, tn)

    peers = [dom_peer(o) for o in OFFSETS]
    peers += [t_peer(k) for k in range(1, g.T)]
    peers += [a_peer(off)[1] for off in a_offs]
    peers += [b_peer(off)[1] for off in b_offs]
    fetches = [
        pltpu.make_async_copy(src, dst, in_sems.at[i])
        for i, (src, dst) in enumerate(
            (
                (x_any, x_ref),
                (wk_any, wall_t.at[0:HD]),
                (wv_any, wall_t.at[HD : 2 * HD]),
                (wq_any, wall_t.at[2 * HD : 3 * HD]),
                (wo_any, wo_pad.at[HD : 2 * HD]),
                (cot_any, cot_ref),
            )
        )
    ]
    for copy in fetches:
        copy.start()
    barrier = pltpu.get_barrier_semaphore()
    for peer in peers:
        pl.semaphore_signal(barrier, inc=1, device_id=peer, device_id_type=MESH)

    def remote(src, dst, ss, rs, peer):
        copy = pltpu.make_async_remote_copy(
            src_ref=src, dst_ref=dst, send_sem=ss, recv_sem=rs, device_id=peer, device_id_type=MESH
        )
        copy.start()
        return copy

    started = []

    fetches[0].wait()
    fetches[1].wait()
    fetches[2].wait()
    for b in range(NBLK):
        rows = slice(b * BLK, (b + 1) * BLK)
        xf = x_ref[rows, :].astype(F32)
        inv = lax.rsqrt(jnp.mean(xf * xf, axis=-1, keepdims=True) + 1e-05)
        unit[rows, :] = (xf * inv).astype(BF16)
    for b in range(NBLK):
        rows = slice(b * BLK, (b + 1) * BLK)
        block = nt(unit[rows, :], wall_t[: 2 * HD, :]).astype(BF16)
        kv_own[b] = block
        pool[b] = block
    for i in range(4):
        for c in range(2):
            kvs[i, c] = kv_own[sb[0, c, i]]
    pl.semaphore_wait(barrier, len(peers))
    kv_copies = []
    for i in (2, 3, 0, 1):
        kv_copies.append(
            remote(kvs.at[i], pool.at[pl.ds(NBLK + 2 * i, 2)], kv_ss.at[i], kv_rs.at[i], dom_peer(OFFSETS[i]))
        )

    wo_pad[0:HD, :] = jnp.zeros((HD, D), BF16)
    wall_t[3 * HD :, :] = jnp.zeros((HD, D), BF16)
    fetches[3].wait()
    fetches[4].wait()
    fetches[5].wait()
    for b in range(NBLK):
        rows = slice(b * BLK, (b + 1) * BLK)
        bm[b, 0:BLK, :] = nt(unit[rows, :], wall_t[2 * HD :, :]).astype(BF16)
        bm[b, BLK : 2 * BLK, :] = nt(cot_ref[rows, :], wo_pad[...]).astype(BF16)
        pool_t[b] = kv_own[b].T
    for f in range(D // BLK):
        cols = slice(f * BLK, (f + 1) * BLK)
        for b in range(NBLK):
            x_t[cols, b * BLK : (b + 1) * BLK] = x_ref[b * BLK : (b + 1) * BLK, cols].T
        wo_t[cols, :] = wo_pad[HD : 2 * HD, cols].T
        wall[cols, :] = wall_t[:, cols].T
    square = jnp.zeros((1, ROWS), F32)
    for f in range(D // BLK):
        part = x_t[f * BLK : (f + 1) * BLK, :].astype(F32)
        square = square + jnp.sum(part * part, axis=0, keepdims=True)
    inv_lane = lax.rsqrt(square * (1.0 / D) + 1e-05)
    inv_row[...] = inv_lane

    for copy in kv_copies:
        copy.wait_recv()
    for p in range(NBLK, 3 * NBLK):
        pool_t[p] = pool[p].T

    for b in range(NBLK):
        lists = [nb[b, n] for n in range(3)]
        kv_sel = jnp.concatenate([pool[b]] + [pool[i] for i in lists], axis=0)
        kv_sel_t = jnp.concatenate([pool_t[b]] + [pool_t[i] for i in lists], axis=1)
        both = nt(kv_sel, bm[b])
        scores = both[:, :BLK]
        prob_grad = both[:, BLK:]
        powers = jnp.exp2((scores - jnp.max(scores, axis=0, keepdims=True)) * EXP_SCALE)
        weights = powers * (1.0 / jnp.sum(powers, axis=0, keepdims=True))
        inner = jnp.sum(weights * prob_grad, axis=0, keepdims=True)
        score_low = (weights * (prob_grad - inner) * SHRINK).astype(BF16)
        pair = jnp.concatenate([score_low, weights.astype(BF16)], axis=1)
        grads = nn(pair, bm[b])
        for n in range(4):
            cg[4 * b + n] = grads[n * BLK : (n + 1) * BLK, :]
        outs = nn(kv_sel_t, pair)
        cols = slice(b * BLK, (b + 1) * BLK)
        qg_t[:, cols] = outs[0:HD, 0:BLK].astype(BF16)
        mix_t[:, cols] = outs[HD : 2 * HD, BLK : 2 * BLK].astype(BF16)

    def listed_sum(p, start):
        total = start
        for b in range(NBLK):
            for n in range(3):
                term = jnp.where(nb[b, n] == p, cg[4 * b + n + 1], 0.0)
                total = term if total is None else total + term
        return total

    ret_copies = []
    for i in (2, 3, 0, 1):
        for c in range(2):
            ret_s[i, c] = listed_sum(NBLK + 2 * i + c, None).astype(BF16)
        ret_copies.append(
            remote(ret_s.at[i], ret_r.at[i], ret_ss.at[i], ret_rs.at[i], dom_peer(-OFFSETS[i]))
        )

    for k in range(g.T):
        us[k] = nn(wo_t[k * g.SLAB : (k + 1) * g.SLAB, :], mix_t[...]).astype(BF16)
    u_copies = []
    for k in range(1, g.T):
        u_copies.append(
            remote(us.at[t_index(k)], ur.at[k - 1], u_ss.at[k - 1], u_rs.at[k - 1], t_peer(k))
        )

    def scatter_a(pay, rsa, ss, rs):
        copies = []
        for k, off in enumerate(a_offs):
            index, peer = a_peer(off)
            copies.append(remote(pay.at[index], rsa.at[k], ss.at[k], rs.at[k], peer))
        return copies

    def spread_b(copies, pay, rsa, bb, ss, rs):
        total = pay[my_a].astype(F32)
        for k, copy in enumerate(copies):
            copy.wait_recv()
            total = total + rsa[k].astype(F32)
        bb[my_b] = total.astype(BF16)
        copies = []
        for k, off in enumerate(b_offs):
            copies.append(remote(bb.at[my_b], bb.at[my_b], ss.at[k], rs.at[k], b_peer(off)[1]))
        return copies

    def gather_a(copies, bb, aga, ss, rs):
        for copy in copies:
            copy.wait_recv()
        total = bb[0].astype(F32)
        for j in range(1, g.NB):
            total = total + bb[j].astype(F32)
        aga[my_a] = total.astype(BF16)
        copies = []
        for k, off in enumerate(a_offs):
            copies.append(remote(aga.at[my_a], aga.at[my_a], ss.at[k], rs.at[k], a_peer(off)[1]))
        return copies

    grad_q = nn(qg_t[...], unit[...])
    grad_o = nn(mix_t[...], cot_ref[...])
    lane_blocks = D // BLK
    for a in range(g.NA):
        r, c = a // lane_blocks, a % lane_blocks
        row = r * g.CR
        cols = slice(c * BLK, (c + 1) * BLK)
        if row < HD:
            pay1[a] = grad_q[row : row + g.CR, cols].astype(BF16)
        else:
            pay1[a] = grad_o[row - HD : row - HD + g.CR, cols].astype(BF16)
    a1 = scatter_a(pay1, rsa1, a1_ss, a1_rs)
    started += a1

    for j in range(NBLK):
        own[j] = listed_sum(j, cg[4 * j])
    for b in range(NBLK):
        rows = slice(b * BLK, (b + 1) * BLK)
        query_grad = qg_t[:, rows].astype(F32).T.astype(BF16)
        xx[rows, 2 * HD :] = jnp.concatenate([query_grad, jnp.zeros((BLK, HD), BF16)], axis=1)

    b1 = spread_b(a1, pay1, rsa1, bb1, b1_ss, b1_rs)
    started += b1

    for copy in ret_copies:
        copy.wait_recv()
    for j in range(NBLK):
        total = own[j]
        for i in range(4):
            for c in range(2):
                total = total + jnp.where(sb[0, c, i] == j, ret_r[i, c].astype(F32), 0.0)
        total = total.astype(BF16)
        xx[j * BLK : (j + 1) * BLK, : 2 * HD] = total
        kvg_t[:, j * BLK : (j + 1) * BLK] = total.T

    grad_kv = nn(kvg_t[...], unit[...])
    for a in range(g.NA):
        r, c = a // lane_blocks, a % lane_blocks
        pay2[a] = grad_kv[r * g.CR : (r + 1) * g.CR, c * BLK : (c + 1) * BLK].astype(BF16)
    a2 = scatter_a(pay2, rsa2, a2_ss, a2_rs)
    started += a2

    for k in range(g.T):
        rows = slice(k * g.SLAB, (k + 1) * g.SLAB)
        ts[k] = nt(wall[rows, :], xx[...]).astype(BF16)
    t_copies = []
    for k in range(1, g.T):
        t_copies.append(
            remote(ts.at[t_index(k)], tr.at[k - 1], t_ss.at[k - 1], t_rs.at[k - 1], t_peer(k))
        )
    dots = jnp.zeros((1, ROWS), F32)
    for k in range(g.T):
        rows = slice(k * g.SLAB, (k + 1) * g.SLAB)
        dots = dots + jnp.sum(ts[k].astype(F32) * x_t[rows, :].astype(F32), axis=0, keepdims=True)
    rd_s[...] = dots
    d_copies = []
    for k in range(1, g.T):
        d_copies.append(remote(rd_s, rd_r.at[k - 1], d_ss.at[k - 1], d_rs.at[k - 1], t_peer(k)))

    b2 = spread_b(a2, pay2, rsa2, bb2, b2_ss, b2_rs)
    ga1 = gather_a(b1, bb1, aga1, ga1_ss, ga1_rs)

    total = us[tn].astype(F32)
    for k, copy in enumerate(u_copies):
        copy.wait_recv()
        total = total + ur[k].astype(F32)
    upd_ref[...] = total.astype(BF16)

    total = ts[tn].astype(F32)
    for k, copy in enumerate(t_copies):
        copy.wait_recv()
        total = total + tr[k].astype(F32)
    for k, copy in enumerate(d_copies):
        copy.wait_recv()
        dots = dots + rd_r[k]
    inv_lane = inv_row[...]
    slab = x_t[pl.ds(pl.multiple_of(tn * g.SLAB, g.SLAB), g.SLAB), :].astype(F32) * inv_lane
    row_mean = dots * inv_lane * (1.0 / D)
    br_ref[...] = (inv_lane * (total - slab * row_mean)).astype(BF16)

    ga2 = gather_a(b2, bb2, aga2, ga2_ss, ga2_rs)

    for copy in ga1:
        copy.wait_recv()
    for a in range(g.NA):
        r, c = a // lane_blocks, a % lane_blocks
        w_ref[0, r * g.CR : (r + 1) * g.CR, c * BLK : (c + 1) * BLK] = aga1[a].astype(F32) * g.factor
    for copy in ga2:
        copy.wait_recv()
    for a in range(g.NA):
        r, c = a // lane_blocks, a % lane_blocks
        w_ref[1, r * g.CR : (r + 1) * g.CR, c * BLK : (c + 1) * BLK] = aga2[a].astype(F32) * g.factor

    started += kv_copies + ret_copies + u_copies + t_copies + d_copies
    started += b2 + ga1 + ga2
    for copy in started:
        copy.wait_send()


def write_kernel(upd, br, w, o0, o1, o2, o3, o4, o5, sems):
    pairs = [
        (upd, o0), (br, o1),
        (w.at[0, 0:HD], o2), (w.at[1, 0:HD], o3), (w.at[1, HD : 2 * HD], o4), (w.at[0, HD : 2 * HD], o5),
    ]
    copies = [pltpu.make_async_copy(src, dst, sems.at[i]) for i, (src, dst) in enumerate(pairs)]
    for copy in copies:
        copy.start()
    for copy in copies:
        copy.wait()


def write_out(g, upd, br, w):
    slab = jax.ShapeDtypeStruct((g.SLAB, ROWS), BF16)
    grad = jax.ShapeDtypeStruct((HD, D), F32)
    return pl.pallas_call(
        write_kernel,
        out_shape=[slab, slab, grad, grad, grad, grad],
        in_specs=[pl.BlockSpec(memory_space=pl.ANY)] * 3,
        out_specs=[pl.BlockSpec(memory_space=pltpu.HBM)] * 6,
        scratch_shapes=[pltpu.SemaphoreType.DMA((6,))],
        compiler_params=pltpu.CompilerParams(vmem_limit_bytes=4 * 1024 * 1024),
        name="write",
    )(upd, br, w)


def body(g, states, w_query, w_key, w_value, w_out, send_blocks, neighbor_blocks, cotangent):
    vmem = pl.BlockSpec(memory_space=pltpu.VMEM)
    smem = pl.BlockSpec(memory_space=pltpu.SMEM)
    sem = pltpu.SemaphoreType.DMA
    blocks = (BLK, 2 * HD)
    reduce_bufs = [
        pltpu.VMEM((g.NA, g.CR, 128), BF16),
        pltpu.VMEM((max(g.NA - 1, 1), g.CR, 128), BF16),
        pltpu.VMEM((g.NB, g.CR, 128), BF16),
        pltpu.VMEM((g.NA, g.CR, 128), BF16),
    ]
    na, nbb, nt_ = max(g.NA - 1, 1), max(g.NB - 1, 1), max(g.T - 1, 1)
    reduce_sems = [sem((n,)) for n in (na, na, nbb, nbb, na, na)]
    out = pl.pallas_call(
        functools.partial(kernel, g),
        out_shape=[
            jax.ShapeDtypeStruct((g.SLAB, ROWS), BF16),
            jax.ShapeDtypeStruct((g.SLAB, ROWS), BF16),
            jax.ShapeDtypeStruct((2, 2 * HD, D), F32),
        ],
        in_specs=[smem, smem] + [pl.BlockSpec(memory_space=pltpu.HBM)] * 6,
        out_specs=[vmem] * 3,
        scratch_shapes=[
            pltpu.VMEM((ROWS, D), BF16),
            pltpu.VMEM((ROWS, D), BF16),
            sem((6,)),
            pltpu.VMEM((ROWS, D), BF16),
            pltpu.VMEM((D, ROWS), BF16),
            pltpu.VMEM((4 * HD, D), BF16),
            pltpu.VMEM((D, 4 * HD), BF16),
            pltpu.VMEM((D, HD), BF16),
            pltpu.VMEM((2 * HD, D), BF16),
            pltpu.VMEM((1, ROWS), F32),
            pltpu.VMEM((NBLK, 2 * BLK, 2 * HD), BF16),
            pltpu.VMEM((NBLK,) + blocks, BF16),
            pltpu.VMEM((3 * NBLK,) + blocks, BF16),
            pltpu.VMEM((3 * NBLK,) + blocks, BF16),
            pltpu.VMEM((4, 2) + blocks, BF16),
            pltpu.VMEM((4 * NBLK,) + blocks, F32),
            pltpu.VMEM((HD, ROWS), BF16),
            pltpu.VMEM((HD, ROWS), BF16),
            pltpu.VMEM((ROWS, 4 * HD), BF16),
            pltpu.VMEM((NBLK,) + blocks, F32),
            pltpu.VMEM((4, 2) + blocks, BF16),
            pltpu.VMEM((4, 2) + blocks, BF16),
            pltpu.VMEM((g.T, g.SLAB, ROWS), BF16),
            pltpu.VMEM((nt_, g.SLAB, ROWS), BF16),
            pltpu.VMEM((g.T, g.SLAB, ROWS), BF16),
            pltpu.VMEM((nt_, g.SLAB, ROWS), BF16),
            pltpu.VMEM((1, ROWS), F32),
            pltpu.VMEM((nt_, 1, ROWS), F32),
            pltpu.VMEM((2 * HD, ROWS), BF16),
        ]
        + reduce_bufs
        + reduce_bufs
        + [sem((4,))] * 4
        + [sem((nt_,))] * 6
        + reduce_sems
        + reduce_sems,
        compiler_params=pltpu.CompilerParams(
            collective_id=0, has_side_effects=True, vmem_limit_bytes=40 * 1024 * 1024
        ),
        name="layer",
    )(
        jnp.swapaxes(send_blocks, 1, 2), neighbor_blocks, states[0], w_query.T, w_key.T, w_value.T, w_out, cotangent[0]
    )
    done = write_out(g, *out)
    return (done[0].T[None], done[1].T[None], done[2].T, done[3].T, done[4].T, done[5])


def solution(mesh):
    placed = (
        P("dp", "dom", None),
        P(None, "tensor"),
        P(None, "tensor"),
        P(None, "tensor"),
        P("tensor", None),
        P("dom", None, None),
        P("dom", None),
        P("dp", "dom", None),
    )
    g = Sizes(mesh.shape["dp"], mesh.shape["dom"], mesh.shape["tensor"])
    return jax.shard_map(
        functools.partial(body, g),
        mesh=mesh,
        in_specs=placed,
        out_specs=(
            P("dp", "dom", "tensor"),
            P("dp", "dom", "tensor"),
            P(None, "tensor"),
            P(None, "tensor"),
            P(None, "tensor"),
            P("tensor", None),
        ),
        check_vma=False,
    )
```

```python
import functools
import math

import jax
import jax.numpy as jnp
from jax import lax
from jax.experimental import pallas as pl
from jax.experimental.pallas import tpu as pltpu
from jax.sharding import PartitionSpec as P

BLK = 128
HD = 64
D = 512
NBLK = 4
ROWS = NBLK * BLK
OFFSETS = (1, -1, 2, -2)
NY = 4
F32 = jnp.float32
BF16 = jnp.bfloat16
MESH = pl.DeviceIdType.MESH
EXP_SCALE = (1.0 / math.sqrt(HD)) / math.log(2.0)
SHRINK = 1.0 / math.sqrt(HD)


def nn(a, b):
    return lax.dot_general(a, b, (((1,), (0,)), ((), ())), preferred_element_type=F32)


def nt(a, b):
    return lax.dot_general(a, b, (((1,), (1,)), ((), ())), preferred_element_type=F32)


class Sizes:
    def __init__(self, dp, dom, t):
        self.DP, self.DOM, self.T = dp, dom, t
        nz = dom // NY
        self.ZR = min(4, nz)
        self.ZQ = nz // self.ZR
        self.NA = NY * self.ZR
        self.NB = self.ZQ * dp
        self.CR = 512 // self.NA
        self.SLAB = D // t
        self.factor = 1.0 / math.sqrt(dp * dom * ROWS)


def kernel(
    g,
    sb_any, nb_any, x_any, wq_any, wk_any, wv_any, wo_any, cot_any,
    upd_ref, br_ref, w_ref,
    sb, nb, x_ref, cot_ref, in_sems, unit_b, x_t, wall_t, wall, wo_t, wo_pad, inv_row, bm, kv_own, pool, pool_t, kvs,
    cg, mix_t, qg_t, xx, own, ret_s, ret_r,
    us, ur, ts, tr, rd_s, rd_r, kvg_t, rows_s, rows_r, gkv,
    pay1, rsa1, bb1, aga1, pay2, rsa2, bb2, aga2,
    kv_ss, kv_rs, ret_ss, ret_rs, row_ss, row_rs, u_ss, u_rs, t_ss, t_rs, d_ss, d_rs,
    a1_ss, a1_rs, b1_ss, b1_rs, ga1_ss, ga1_rs,
    a2_ss, a2_rs, b2_ss, b2_rs, ga2_ss, ga2_rs,
):
    dp = lax.axis_index("dp")
    dom = lax.axis_index("dom")
    tn = lax.axis_index("tensor")
    y = lax.rem(dom, NY)
    z = dom // NY
    zr = lax.rem(z, g.ZR)
    zq = z // g.ZR
    my_a = y * g.ZR + zr
    my_b = dp * g.ZQ + zq

    def dom_peer(o):
        return (dp, lax.rem(dom + (o + g.DOM), g.DOM), tn)

    def t_index(k):
        return lax.rem(tn + k, g.T)

    def t_peer(k):
        return (dp, dom, t_index(k))

    a_offs = [(dy, dz) for dy in range(NY) for dz in range(g.ZR)][1:]
    b_offs = [(dd, dq) for dd in range(g.DP) for dq in range(g.ZQ)][1:]

    def a_peer(off):
        y2 = lax.rem(y + off[0], NY)
        r2 = lax.rem(zr + off[1], g.ZR)
        return y2 * g.ZR + r2, (dp, (zq * g.ZR + r2) * NY + y2, tn)

    def b_peer(off):
        d2 = lax.rem(dp + off[0], g.DP)
        q2 = lax.rem(zq + off[1], g.ZQ)
        return d2 * g.ZQ + q2, (d2, (q2 * g.ZR + zr) * NY + y, tn)

    def far(size, d):
        return min(d, size - d)

    b_offs.sort(key=lambda off: -(16 * off[0] + 4 * off[1] if not off[0] else 16 - 4 * off[1]))
    a_offs.sort(key=lambda off: -(far(NY, off[0]) + (3 if off[1] else 0)))
    peers = [dom_peer(o) for o in OFFSETS]
    peers += [t_peer(k) for k in range(1, g.T)]
    peers += [a_peer(off)[1] for off in a_offs]
    peers += [b_peer(off)[1] for off in b_offs]
    fetches = [
        pltpu.make_async_copy(src, dst, in_sems.at[i])
        for i, (src, dst) in enumerate(
            (
                (x_any, x_ref),
                (wk_any, wall_t.at[0:HD]),
                (wv_any, wall_t.at[HD : 2 * HD]),
                (wq_any, wall_t.at[2 * HD : 3 * HD]),
                (wo_any, wo_pad.at[HD : 2 * HD]),
                (cot_any, cot_ref),
                (sb_any, sb),
                (nb_any, nb),
            )
        )
    ]
    for copy in fetches:
        copy.start()
    barrier = pltpu.get_barrier_semaphore()
    for peer in peers:
        pl.semaphore_signal(barrier, inc=1, device_id=peer, device_id_type=MESH)

    def remote(src, dst, ss, rs, peer):
        copy = pltpu.make_async_remote_copy(
            src_ref=src, dst_ref=dst, send_sem=ss, recv_sem=rs, device_id=peer, device_id_type=MESH
        )
        copy.start()
        return copy

    started = []

    fetches[0].wait()
    fetches[1].wait()
    fetches[2].wait()
    for b in range(NBLK):
        rows = slice(b * BLK, (b + 1) * BLK)
        xf = x_ref[rows, :].astype(F32)
        inv = lax.rsqrt(jnp.mean(xf * xf, axis=-1, keepdims=True) + 1e-05)
        unit_b[b] = (xf * inv).astype(BF16)
    for b in range(NBLK):
        rows = slice(b * BLK, (b + 1) * BLK)
        block = nt(unit_b[b], wall_t[: 2 * HD, :]).astype(BF16)
        kv_own[b] = block
        pool[b] = block
    fetches[6].wait()
    fetches[7].wait()
    for i in range(4):
        for c in range(2):
            kvs[i, c] = kv_own[sb[0, c, i]]
    pl.semaphore_wait(barrier, len(peers))
    kv_copies = []
    for i in (2, 3, 0, 1):
        kv_copies.append(
            remote(kvs.at[i], pool.at[pl.ds(NBLK + 2 * i, 2)], kv_ss.at[i], kv_rs.at[i], dom_peer(OFFSETS[i]))
        )

    def send_wraps(i):
        there = dom + OFFSETS[i]
        return jnp.logical_or(there < 0, there >= g.DOM)

    def recv_wraps(i):
        there = dom - OFFSETS[i]
        return jnp.logical_or(there < 0, there >= g.DOM)

    def row_copy(i):
        return pltpu.make_async_remote_copy(
            src_ref=rows_s.at[i], dst_ref=rows_r.at[i], send_sem=row_ss.at[i], recv_sem=row_rs.at[i],
            device_id=dom_peer(OFFSETS[i]), device_id_type=MESH,
        )

    for i in (2, 3, 0, 1):
        @pl.when(send_wraps(i))
        def _(i=i):
            for c in range(2):
                rows_s[i, c] = unit_b[sb[0, c, i]]
            row_copy(i).start()

    wo_pad[0:HD, :] = jnp.zeros((HD, D), BF16)
    wall_t[3 * HD :, :] = jnp.zeros((HD, D), BF16)
    fetches[3].wait()
    fetches[4].wait()
    fetches[5].wait()
    for b in range(NBLK):
        rows = slice(b * BLK, (b + 1) * BLK)
        bm[b, 0:BLK, :] = nt(unit_b[b], wall_t[2 * HD :, :]).astype(BF16)
        bm[b, BLK : 2 * BLK, :] = nt(cot_ref[rows, :], wo_pad[...]).astype(BF16)
        pool_t[b] = kv_own[b].T
    for f in range(D // BLK):
        cols = slice(f * BLK, (f + 1) * BLK)
        for b in range(NBLK):
            x_t[cols, b * BLK : (b + 1) * BLK] = x_ref[b * BLK : (b + 1) * BLK, cols].T
        wo_t[cols, :] = wo_pad[HD : 2 * HD, cols].T
        wall[cols, :] = wall_t[:, cols].T
    square = jnp.zeros((1, ROWS), F32)
    for f in range(D // BLK):
        part = x_t[f * BLK : (f + 1) * BLK, :].astype(F32)
        square = square + jnp.sum(part * part, axis=0, keepdims=True)
    inv_lane = lax.rsqrt(square * (1.0 / D) + 1e-05)
    inv_row[...] = inv_lane

    for copy in kv_copies:
        copy.wait_recv()
    for p in range(NBLK, 3 * NBLK):
        pool_t[p] = pool[p].T

    for b in range(NBLK):
        lists = [nb[b, n] for n in range(3)]
        kv_sel = jnp.concatenate([pool[b]] + [pool[i] for i in lists], axis=0)
        kv_sel_t = jnp.concatenate([pool_t[b]] + [pool_t[i] for i in lists], axis=1)
        both = nt(kv_sel, bm[b])
        scores = both[:, :BLK]
        prob_grad = both[:, BLK:]
        powers = jnp.exp2((scores - jnp.max(scores, axis=0, keepdims=True)) * EXP_SCALE)
        weights = powers * (1.0 / jnp.sum(powers, axis=0, keepdims=True))
        inner = jnp.sum(weights * prob_grad, axis=0, keepdims=True)
        score_low = (weights * (prob_grad - inner) * SHRINK).astype(BF16)
        pair = jnp.concatenate([score_low, weights.astype(BF16)], axis=1)
        grads = nn(pair, bm[b])
        for n in range(4):
            cg[4 * b + n] = grads[n * BLK : (n + 1) * BLK, :]
        outs = nn(kv_sel_t, pair)
        cols = slice(b * BLK, (b + 1) * BLK)
        qg_t[:, cols] = outs[0:HD, 0:BLK].astype(BF16)
        mix_t[:, cols] = outs[HD : 2 * HD, BLK : 2 * BLK].astype(BF16)

    def listed_sum(p, start):
        total = start
        for b in range(NBLK):
            for n in range(3):
                term = jnp.where(nb[b, n] == p, cg[4 * b + n + 1], 0.0)
                total = term if total is None else total + term
        return total

    ret_copies = []
    for i in (2, 3, 0, 1):
        for c in range(2):
            ret_s[i, c] = listed_sum(NBLK + 2 * i + c, None).astype(BF16)
        ret_copies.append(
            remote(ret_s.at[i], ret_r.at[i], ret_ss.at[i], ret_rs.at[i], dom_peer(-OFFSETS[i]))
        )

    for k in range(g.T):
        us[k] = nn(wo_t[k * g.SLAB : (k + 1) * g.SLAB, :], mix_t[...]).astype(BF16)
    u_copies = []
    for k in range(1, g.T):
        u_copies.append(
            remote(us.at[t_index(k)], ur.at[k - 1], u_ss.at[k - 1], u_rs.at[k - 1], t_peer(k))
        )

    def scatter_a(pay, rsa, ss, rs):
        copies = []
        for k, off in enumerate(a_offs):
            index, peer = a_peer(off)
            copies.append(remote(pay.at[index], rsa.at[k], ss.at[k], rs.at[k], peer))
        return copies

    def spread_b(copies, pay, rsa, bb, ss, rs):
        total = pay[my_a].astype(F32)
        for k, copy in enumerate(copies):
            copy.wait_recv()
            total = total + rsa[k].astype(F32)
        bb[my_b] = total.astype(BF16)
        copies = []
        for k, off in enumerate(b_offs):
            copies.append(remote(bb.at[my_b], bb.at[my_b], ss.at[k], rs.at[k], b_peer(off)[1]))
        return copies

    def gather_a(copies, bb, aga, ss, rs):
        for copy in copies:
            copy.wait_recv()
        total = bb[0].astype(F32)
        for j in range(1, g.NB):
            total = total + bb[j].astype(F32)
        aga[my_a] = total.astype(BF16)
        copies = []
        for k, off in enumerate(a_offs):
            copies.append(remote(aga.at[my_a], aga.at[my_a], ss.at[k], rs.at[k], a_peer(off)[1]))
        return copies

    unit = unit_b[...].reshape(ROWS, D)
    grad_q = nn(qg_t[...], unit)
    grad_o = nn(mix_t[...], cot_ref[...])
    lane_blocks = D // BLK
    for a in range(g.NA):
        r, c = a // lane_blocks, a % lane_blocks
        row = r * g.CR
        cols = slice(c * BLK, (c + 1) * BLK)
        if row < HD:
            pay1[a] = grad_q[row : row + g.CR, cols].astype(BF16)
        else:
            pay1[a] = grad_o[row - HD : row - HD + g.CR, cols].astype(BF16)
    a1 = scatter_a(pay1, rsa1, a1_ss, a1_rs)
    started += a1

    for j in range(NBLK):
        own[j] = listed_sum(j, cg[4 * j])
    for b in range(NBLK):
        rows = slice(b * BLK, (b + 1) * BLK)
        query_grad = qg_t[:, rows].astype(F32).T.astype(BF16)
        xx[rows, 2 * HD :] = jnp.concatenate([query_grad, jnp.zeros((BLK, HD), BF16)], axis=1)

    b1 = spread_b(a1, pay1, rsa1, bb1, b1_ss, b1_rs)
    started += b1

    def returned(i, c, j):
        return jnp.where(sb[0, c, i] == j, ret_r[i, c].astype(F32), 0.0)

    for i, copy in zip((2, 3, 0, 1), ret_copies):
        @pl.when(jnp.logical_not(send_wraps(i)))
        def _(i=i, copy=copy):
            copy.wait_recv()
            for j in range(NBLK):
                own[j] = own[j] + (returned(i, 0, j) + returned(i, 1, j))
    for j in range(NBLK):
        kvg_t[:, j * BLK : (j + 1) * BLK] = own[j].astype(BF16).T
    gkv[...] = nn(kvg_t[...], unit)
    for i in (2, 3, 0, 1):
        @pl.when(recv_wraps(i))
        def _(i=i):
            row_copy(i).wait_recv()
            for c in range(2):
                gkv[...] += nn(ret_s[i, c].T, rows_r[i, c])
    for a in range(g.NA):
        r, c = a // lane_blocks, a % lane_blocks
        pay2[a] = gkv[r * g.CR : (r + 1) * g.CR, c * BLK : (c + 1) * BLK].astype(BF16)
    a2 = scatter_a(pay2, rsa2, a2_ss, a2_rs)
    started += a2
    b2 = spread_b(a2, pay2, rsa2, bb2, b2_ss, b2_rs)

    for i, copy in zip((2, 3, 0, 1), ret_copies):
        @pl.when(send_wraps(i))
        def _(i=i, copy=copy):
            copy.wait_recv()
            for j in range(NBLK):
                own[j] = own[j] + (returned(i, 0, j) + returned(i, 1, j))
    for j in range(NBLK):
        xx[j * BLK : (j + 1) * BLK, : 2 * HD] = own[j].astype(BF16)

    for k in range(g.T):
        rows = slice(k * g.SLAB, (k + 1) * g.SLAB)
        ts[k] = nt(wall[rows, :], xx[...]).astype(BF16)
    t_copies = []
    for k in range(1, g.T):
        t_copies.append(
            remote(ts.at[t_index(k)], tr.at[k - 1], t_ss.at[k - 1], t_rs.at[k - 1], t_peer(k))
        )
    dots = jnp.zeros((1, ROWS), F32)
    for k in range(g.T):
        rows = slice(k * g.SLAB, (k + 1) * g.SLAB)
        dots = dots + jnp.sum(ts[k].astype(F32) * x_t[rows, :].astype(F32), axis=0, keepdims=True)
    rd_s[...] = dots
    d_copies = []
    for k in range(1, g.T):
        d_copies.append(remote(rd_s, rd_r.at[k - 1], d_ss.at[k - 1], d_rs.at[k - 1], t_peer(k)))

    ga1 = gather_a(b1, bb1, aga1, ga1_ss, ga1_rs)

    total = us[tn].astype(F32)
    for k, copy in enumerate(u_copies):
        copy.wait_recv()
        total = total + ur[k].astype(F32)
    upd_ref[...] = total.astype(BF16)

    total = ts[tn].astype(F32)
    for k, copy in enumerate(t_copies):
        copy.wait_recv()
        total = total + tr[k].astype(F32)
    for k, copy in enumerate(d_copies):
        copy.wait_recv()
        dots = dots + rd_r[k]
    inv_lane = inv_row[...]
    slab = x_t[pl.ds(pl.multiple_of(tn * g.SLAB, g.SLAB), g.SLAB), :].astype(F32) * inv_lane
    row_mean = dots * inv_lane * (1.0 / D)
    br_ref[...] = (inv_lane * (total - slab * row_mean)).astype(BF16)

    ga2 = gather_a(b2, bb2, aga2, ga2_ss, ga2_rs)

    for copy in ga1:
        copy.wait_recv()
    for a in range(g.NA):
        r, c = a // lane_blocks, a % lane_blocks
        w_ref[0, r * g.CR : (r + 1) * g.CR, c * BLK : (c + 1) * BLK] = aga1[a].astype(F32) * g.factor
    for copy in ga2:
        copy.wait_recv()
    for a in range(g.NA):
        r, c = a // lane_blocks, a % lane_blocks
        w_ref[1, r * g.CR : (r + 1) * g.CR, c * BLK : (c + 1) * BLK] = aga2[a].astype(F32) * g.factor

    started += kv_copies + ret_copies + u_copies + t_copies + d_copies
    started += b2 + ga1 + ga2
    for copy in started:
        copy.wait_send()
    for i in range(4):
        @pl.when(send_wraps(i))
        def _(i=i):
            row_copy(i).wait_send()


def write_kernel(upd, br, w, o0, o1, o2, o3, o4, o5, sems):
    pairs = [
        (upd, o0), (br, o1),
        (w.at[0, 0:HD], o2), (w.at[1, 0:HD], o3), (w.at[1, HD : 2 * HD], o4), (w.at[0, HD : 2 * HD], o5),
    ]
    copies = [pltpu.make_async_copy(src, dst, sems.at[i]) for i, (src, dst) in enumerate(pairs)]
    for copy in copies:
        copy.start()
    for copy in copies:
        copy.wait()


def write_out(g, upd, br, w):
    slab = jax.ShapeDtypeStruct((g.SLAB, ROWS), BF16)
    grad = jax.ShapeDtypeStruct((HD, D), F32)
    return pl.pallas_call(
        write_kernel,
        out_shape=[slab, slab, grad, grad, grad, grad],
        in_specs=[pl.BlockSpec(memory_space=pl.ANY)] * 3,
        out_specs=[pl.BlockSpec(memory_space=pltpu.HBM)] * 6,
        scratch_shapes=[pltpu.SemaphoreType.DMA((6,))],
        compiler_params=pltpu.CompilerParams(vmem_limit_bytes=4 * 1024 * 1024),
        name="write",
    )(upd, br, w)


def body(g, states, w_query, w_key, w_value, w_out, send_blocks, neighbor_blocks, cotangent):
    vmem = pl.BlockSpec(memory_space=pltpu.VMEM)
    sem = pltpu.SemaphoreType.DMA
    blocks = (BLK, 2 * HD)
    reduce_bufs = [
        pltpu.VMEM((g.NA, g.CR, 128), BF16),
        pltpu.VMEM((max(g.NA - 1, 1), g.CR, 128), BF16),
        pltpu.VMEM((g.NB, g.CR, 128), BF16),
        pltpu.VMEM((g.NA, g.CR, 128), BF16),
    ]
    na, nbb, nt_ = max(g.NA - 1, 1), max(g.NB - 1, 1), max(g.T - 1, 1)
    reduce_sems = [sem((n,)) for n in (na, na, nbb, nbb, na, na)]
    inputs = (
        jnp.swapaxes(send_blocks, 1, 2), neighbor_blocks, states[0],
        w_query.T, w_key.T, w_value.T, w_out, cotangent[0],
    )
    out = pl.pallas_call(
        functools.partial(kernel, g),
        out_shape=[
            jax.ShapeDtypeStruct((g.SLAB, ROWS), BF16),
            jax.ShapeDtypeStruct((g.SLAB, ROWS), BF16),
            jax.ShapeDtypeStruct((2, 2 * HD, D), F32),
        ],
        in_specs=[pl.BlockSpec(memory_space=pltpu.HBM)] * 8,
        out_specs=[vmem] * 3,
        scratch_shapes=[
            pltpu.SMEM((1, 2, 4), jnp.int32),
            pltpu.SMEM((NBLK, 3), jnp.int32),
            pltpu.VMEM((ROWS, D), BF16),
            pltpu.VMEM((ROWS, D), BF16),
            sem((8,)),
            pltpu.VMEM((NBLK, BLK, D), BF16),
            pltpu.VMEM((D, ROWS), BF16),
            pltpu.VMEM((4 * HD, D), BF16),
            pltpu.VMEM((D, 4 * HD), BF16),
            pltpu.VMEM((D, HD), BF16),
            pltpu.VMEM((2 * HD, D), BF16),
            pltpu.VMEM((1, ROWS), F32),
            pltpu.VMEM((NBLK, 2 * BLK, 2 * HD), BF16),
            pltpu.VMEM((NBLK,) + blocks, BF16),
            pltpu.VMEM((3 * NBLK,) + blocks, BF16),
            pltpu.VMEM((3 * NBLK,) + blocks, BF16),
            pltpu.VMEM((4, 2) + blocks, BF16),
            pltpu.VMEM((4 * NBLK,) + blocks, F32),
            pltpu.VMEM((HD, ROWS), BF16),
            pltpu.VMEM((HD, ROWS), BF16),
            pltpu.VMEM((ROWS, 4 * HD), BF16),
            pltpu.VMEM((NBLK,) + blocks, F32),
            pltpu.VMEM((4, 2) + blocks, BF16),
            pltpu.VMEM((4, 2) + blocks, BF16),
            pltpu.VMEM((g.T, g.SLAB, ROWS), BF16),
            pltpu.VMEM((nt_, g.SLAB, ROWS), BF16),
            pltpu.VMEM((g.T, g.SLAB, ROWS), BF16),
            pltpu.VMEM((nt_, g.SLAB, ROWS), BF16),
            pltpu.VMEM((1, ROWS), F32),
            pltpu.VMEM((nt_, 1, ROWS), F32),
            pltpu.VMEM((2 * HD, ROWS), BF16),
            pltpu.VMEM((4, 2, BLK, D), BF16),
            pltpu.VMEM((4, 2, BLK, D), BF16),
            pltpu.VMEM((2 * HD, D), F32),
        ]
        + reduce_bufs
        + reduce_bufs
        + [sem((4,))] * 6
        + [sem((nt_,))] * 6
        + reduce_sems
        + reduce_sems,
        compiler_params=pltpu.CompilerParams(
            collective_id=0, has_side_effects=True, vmem_limit_bytes=40 * 1024 * 1024
        ),
        name="layer",
    )(
        *[pltpu.with_memory_space_constraint(value, pltpu.HBM) for value in inputs]
    )
    done = write_out(g, *out)
    return (done[0].T[None], done[1].T[None], done[2].T, done[3].T, done[4].T, done[5])


def solution(mesh):
    placed = (
        P("dp", "dom", None),
        P(None, "tensor"),
        P(None, "tensor"),
        P(None, "tensor"),
        P("tensor", None),
        P("dom", None, None),
        P("dom", None),
        P("dp", "dom", None),
    )
    g = Sizes(mesh.shape["dp"], mesh.shape["dom"], mesh.shape["tensor"])
    return jax.shard_map(
        functools.partial(body, g),
        mesh=mesh,
        in_specs=placed,
        out_specs=(
            P("dp", "dom", "tensor"),
            P("dp", "dom", "tensor"),
            P(None, "tensor"),
            P(None, "tensor"),
            P(None, "tensor"),
            P("tensor", None),
        ),
        check_vma=False,
    )
```

```python
import functools
import math

import jax
import jax.numpy as jnp
from jax import lax
from jax.experimental import pallas as pl
from jax.experimental.pallas import tpu as pltpu
from jax.sharding import PartitionSpec as P

BLK = 128
HD = 64
D = 512
NBLK = 4
ROWS = NBLK * BLK
OFFSETS = (1, -1, 2, -2)
NY = 4
F32 = jnp.float32
BF16 = jnp.bfloat16
MESH = pl.DeviceIdType.MESH
EXP_SCALE = (1.0 / math.sqrt(HD)) / math.log(2.0)
SHRINK = 1.0 / math.sqrt(HD)


def nn(a, b):
    return lax.dot_general(a, b, (((1,), (0,)), ((), ())), preferred_element_type=F32)


def nt(a, b):
    return lax.dot_general(a, b, (((1,), (1,)), ((), ())), preferred_element_type=F32)


class Sizes:
    def __init__(self, dp, dom, t):
        self.DP, self.DOM, self.T = dp, dom, t
        nz = dom // NY
        self.ZR = min(4, nz)
        self.ZQ = nz // self.ZR
        self.NA = NY * self.ZR
        self.NB = self.ZQ * dp
        self.CR = 512 // self.NA
        self.SLAB = D // t
        self.factor = 1.0 / math.sqrt(dp * dom * ROWS)


def kernel(
    g,
    sb_any, nb_any, x_any, wq_any, wk_any, wv_any, wo_any, cot_any,
    upd_ref, br_ref, w_ref,
    sb, nb, x_ref, cot_ref, in_sems, unit_b, x_t, wall_t, wall, wo_t, wo_pad, inv_row, bm, kv_own, pool, pool_t, kvs,
    cg, mix_t, qg_t, xx, own, ret_s, ret_r,
    us, ur, ts, tr, rd_s, rd_r, kvg_t, rows_s, rows_r, gkv,
    pay1, rsa1, bb1, aga1, pay2, rsa2, bb2, aga2,
    kv_ss, kv_rs, ret_ss, ret_rs, row_ss, row_rs, pass_ss, pass_rs, u_ss, u_rs, t_ss, t_rs, d_ss, d_rs,
    a1_ss, a1_rs, b1_ss, b1_rs, ga1_ss, ga1_rs,
    a2_ss, a2_rs, b2_ss, b2_rs, ga2_ss, ga2_rs,
):
    dp = lax.axis_index("dp")
    dom = lax.axis_index("dom")
    tn = lax.axis_index("tensor")
    y = lax.rem(dom, NY)
    z = dom // NY
    zr = lax.rem(z, g.ZR)
    zq = z // g.ZR
    my_a = y * g.ZR + zr
    my_b = dp * g.ZQ + zq

    def dom_peer(o):
        return (dp, lax.rem(dom + (o + g.DOM), g.DOM), tn)

    def t_index(k):
        return lax.rem(tn + k, g.T)

    def t_peer(k):
        return (dp, dom, t_index(k))

    a_offs = [(dy, dz) for dy in range(NY) for dz in range(g.ZR)][1:]
    b_offs = [(dd, dq) for dd in range(g.DP) for dq in range(g.ZQ)][1:]

    def a_peer(off):
        y2 = lax.rem(y + off[0], NY)
        r2 = lax.rem(zr + off[1], g.ZR)
        return y2 * g.ZR + r2, (dp, (zq * g.ZR + r2) * NY + y2, tn)

    def b_peer(off):
        d2 = lax.rem(dp + off[0], g.DP)
        q2 = lax.rem(zq + off[1], g.ZQ)
        return d2 * g.ZQ + q2, (d2, (q2 * g.ZR + zr) * NY + y, tn)

    def far(size, d):
        return min(d, size - d)

    b_offs.sort(key=lambda off: -(16 * off[0] + 4 * off[1] if not off[0] else 16 - 4 * off[1]))
    a_offs.sort(key=lambda off: -(far(NY, off[0]) + (3 if off[1] else 0)))
    peers = [dom_peer(o) for o in OFFSETS]
    peers += [t_peer(k) for k in range(1, g.T)]
    peers += [a_peer(off)[1] for off in a_offs]
    peers += [b_peer(off)[1] for off in b_offs]
    fetches = [
        pltpu.make_async_copy(src, dst, in_sems.at[i])
        for i, (src, dst) in enumerate(
            (
                (x_any, x_ref),
                (wk_any, wall_t.at[0:HD]),
                (wv_any, wall_t.at[HD : 2 * HD]),
                (wq_any, wall_t.at[2 * HD : 3 * HD]),
                (wo_any, wo_pad.at[HD : 2 * HD]),
                (cot_any, cot_ref),
                (sb_any, sb),
                (nb_any, nb),
            )
        )
    ]
    for copy in fetches:
        copy.start()
    barrier = pltpu.get_barrier_semaphore()
    for peer in peers:
        pl.semaphore_signal(barrier, inc=1, device_id=peer, device_id_type=MESH)

    def remote(src, dst, ss, rs, peer):
        copy = pltpu.make_async_remote_copy(
            src_ref=src, dst_ref=dst, send_sem=ss, recv_sem=rs, device_id=peer, device_id_type=MESH
        )
        copy.start()
        return copy

    started = []

    fetches[0].wait()
    fetches[1].wait()
    fetches[2].wait()
    for b in range(NBLK):
        rows = slice(b * BLK, (b + 1) * BLK)
        xf = x_ref[rows, :].astype(F32)
        inv = lax.rsqrt(jnp.mean(xf * xf, axis=-1, keepdims=True) + 1e-05)
        unit_b[b] = (xf * inv).astype(BF16)
    for b in range(NBLK):
        rows = slice(b * BLK, (b + 1) * BLK)
        block = nt(unit_b[b], wall_t[: 2 * HD, :]).astype(BF16)
        kv_own[b] = block
        pool[b] = block
    fetches[6].wait()
    fetches[7].wait()
    for i in range(4):
        for c in range(2):
            kvs[i, c] = kv_own[sb[0, c, i]]
    pl.semaphore_wait(barrier, len(peers))
    kv_copies = []
    for i in (2, 3, 0, 1):
        kv_copies.append(
            remote(kvs.at[i], pool.at[pl.ds(NBLK + 2 * i, 2)], kv_ss.at[i], kv_rs.at[i], dom_peer(OFFSETS[i]))
        )

    half = lax.rem(tn, 2)

    def send_wraps(i):
        there = dom + OFFSETS[i]
        return jnp.logical_or(there < 0, there >= g.DOM)

    def recv_wraps(i):
        there = dom - OFFSETS[i]
        return jnp.logical_or(there < 0, there >= g.DOM)

    def row_copy(i):
        return pltpu.make_async_remote_copy(
            src_ref=rows_s.at[i], dst_ref=rows_r.at[i, half], send_sem=row_ss.at[i], recv_sem=row_rs.at[i],
            device_id=dom_peer(OFFSETS[i]), device_id_type=MESH,
        )

    def pass_copy(i):
        return pltpu.make_async_remote_copy(
            src_ref=rows_r.at[i, half], dst_ref=rows_r.at[i, half], send_sem=pass_ss.at[i], recv_sem=pass_rs.at[i],
            device_id=(dp, dom, tn + 1 - 2 * half), device_id_type=MESH,
        )

    for i in (2, 3, 0, 1):
        @pl.when(send_wraps(i))
        def _(i=i):
            rows_s[i] = unit_b[sb[0, half, i]]
            row_copy(i).start()

    wo_pad[0:HD, :] = jnp.zeros((HD, D), BF16)
    wall_t[3 * HD :, :] = jnp.zeros((HD, D), BF16)
    fetches[3].wait()
    fetches[4].wait()
    fetches[5].wait()
    for b in range(NBLK):
        rows = slice(b * BLK, (b + 1) * BLK)
        bm[b, 0:BLK, :] = nt(unit_b[b], wall_t[2 * HD :, :]).astype(BF16)
        bm[b, BLK : 2 * BLK, :] = nt(cot_ref[rows, :], wo_pad[...]).astype(BF16)
        pool_t[b] = kv_own[b].T
    for f in range(D // BLK):
        cols = slice(f * BLK, (f + 1) * BLK)
        for b in range(NBLK):
            x_t[cols, b * BLK : (b + 1) * BLK] = x_ref[b * BLK : (b + 1) * BLK, cols].T
        wo_t[cols, :] = wo_pad[HD : 2 * HD, cols].T
        wall[cols, :] = wall_t[:, cols].T
    square = jnp.zeros((1, ROWS), F32)
    for f in range(D // BLK):
        part = x_t[f * BLK : (f + 1) * BLK, :].astype(F32)
        square = square + jnp.sum(part * part, axis=0, keepdims=True)
    inv_lane = lax.rsqrt(square * (1.0 / D) + 1e-05)
    inv_row[...] = inv_lane

    for copy in kv_copies:
        copy.wait_recv()
    for p in range(NBLK, 3 * NBLK):
        pool_t[p] = pool[p].T

    for b in range(NBLK):
        lists = [nb[b, n] for n in range(3)]
        kv_sel = jnp.concatenate([pool[b]] + [pool[i] for i in lists], axis=0)
        kv_sel_t = jnp.concatenate([pool_t[b]] + [pool_t[i] for i in lists], axis=1)
        both = nt(kv_sel, bm[b])
        scores = both[:, :BLK]
        prob_grad = both[:, BLK:]
        powers = jnp.exp2((scores - jnp.max(scores, axis=0, keepdims=True)) * EXP_SCALE)
        weights = powers * (1.0 / jnp.sum(powers, axis=0, keepdims=True))
        inner = jnp.sum(weights * prob_grad, axis=0, keepdims=True)
        score_low = (weights * (prob_grad - inner) * SHRINK).astype(BF16)
        pair = jnp.concatenate([score_low, weights.astype(BF16)], axis=1)
        grads = nn(pair, bm[b])
        for n in range(4):
            cg[4 * b + n] = grads[n * BLK : (n + 1) * BLK, :]
        outs = nn(kv_sel_t, pair)
        cols = slice(b * BLK, (b + 1) * BLK)
        qg_t[:, cols] = outs[0:HD, 0:BLK].astype(BF16)
        mix_t[:, cols] = outs[HD : 2 * HD, BLK : 2 * BLK].astype(BF16)

    def listed_sum(p, start):
        total = start
        for b in range(NBLK):
            for n in range(3):
                term = jnp.where(nb[b, n] == p, cg[4 * b + n + 1], 0.0)
                total = term if total is None else total + term
        return total

    ret_copies = []
    for i in (2, 3, 0, 1):
        for c in range(2):
            ret_s[i, c] = listed_sum(NBLK + 2 * i + c, None).astype(BF16)
        ret_copies.append(
            remote(ret_s.at[i], ret_r.at[i], ret_ss.at[i], ret_rs.at[i], dom_peer(-OFFSETS[i]))
        )

    for k in range(g.T):
        us[k] = nn(wo_t[k * g.SLAB : (k + 1) * g.SLAB, :], mix_t[...]).astype(BF16)
    u_copies = []
    for k in range(1, g.T):
        u_copies.append(
            remote(us.at[t_index(k)], ur.at[k - 1], u_ss.at[k - 1], u_rs.at[k - 1], t_peer(k))
        )

    def scatter_a(pay, rsa, ss, rs):
        copies = []
        for k, off in enumerate(a_offs):
            index, peer = a_peer(off)
            copies.append(remote(pay.at[index], rsa.at[k], ss.at[k], rs.at[k], peer))
        return copies

    def spread_b(copies, pay, rsa, bb, ss, rs):
        total = pay[my_a].astype(F32)
        for k, copy in enumerate(copies):
            copy.wait_recv()
            total = total + rsa[k].astype(F32)
        bb[my_b] = total.astype(BF16)
        copies = []
        for k, off in enumerate(b_offs):
            copies.append(remote(bb.at[my_b], bb.at[my_b], ss.at[k], rs.at[k], b_peer(off)[1]))
        return copies

    def gather_a(copies, bb, aga, ss, rs):
        for copy in copies:
            copy.wait_recv()
        total = bb[0].astype(F32)
        for j in range(1, g.NB):
            total = total + bb[j].astype(F32)
        aga[my_a] = total.astype(BF16)
        copies = []
        for k, off in enumerate(a_offs):
            copies.append(remote(aga.at[my_a], aga.at[my_a], ss.at[k], rs.at[k], a_peer(off)[1]))
        return copies

    unit = unit_b[...].reshape(ROWS, D)
    grad_q = nn(qg_t[...], unit)
    grad_o = nn(mix_t[...], cot_ref[...])
    lane_blocks = D // BLK
    for a in range(g.NA):
        r, c = a // lane_blocks, a % lane_blocks
        row = r * g.CR
        cols = slice(c * BLK, (c + 1) * BLK)
        if row < HD:
            pay1[a] = grad_q[row : row + g.CR, cols].astype(BF16)
        else:
            pay1[a] = grad_o[row - HD : row - HD + g.CR, cols].astype(BF16)
    a1 = scatter_a(pay1, rsa1, a1_ss, a1_rs)
    started += a1

    for j in range(NBLK):
        own[j] = listed_sum(j, cg[4 * j])
    for b in range(NBLK):
        rows = slice(b * BLK, (b + 1) * BLK)
        query_grad = qg_t[:, rows].astype(F32).T.astype(BF16)
        xx[rows, 2 * HD :] = jnp.concatenate([query_grad, jnp.zeros((BLK, HD), BF16)], axis=1)


    for i in (2, 3, 0, 1):
        @pl.when(recv_wraps(i))
        def _(i=i):
            row_copy(i).wait_recv()
            pass_copy(i).start()

    def returned(i, c, j):
        return jnp.where(sb[0, c, i] == j, ret_r[i, c].astype(F32), 0.0)

    for i, copy in zip((2, 3, 0, 1), ret_copies):
        @pl.when(jnp.logical_not(send_wraps(i)))
        def _(i=i, copy=copy):
            copy.wait_recv()
            for j in range(NBLK):
                own[j] = own[j] + (returned(i, 0, j) + returned(i, 1, j))
    for j in range(NBLK):
        kvg_t[:, j * BLK : (j + 1) * BLK] = own[j].astype(BF16).T
    gkv[...] = nn(kvg_t[...], unit)
    for i in (2, 3, 0, 1):
        @pl.when(recv_wraps(i))
        def _(i=i):
            pass_copy(i).wait_recv()
            for c in range(2):
                gkv[...] += nn(ret_s[i, c].T, rows_r[i, c])
    for a in range(g.NA):
        r, c = a // lane_blocks, a % lane_blocks
        pay2[a] = gkv[r * g.CR : (r + 1) * g.CR, c * BLK : (c + 1) * BLK].astype(BF16)
    a2 = scatter_a(pay2, rsa2, a2_ss, a2_rs)
    started += a2
    b1 = spread_b(a1, pay1, rsa1, bb1, b1_ss, b1_rs)
    started += b1
    b2 = spread_b(a2, pay2, rsa2, bb2, b2_ss, b2_rs)

    for i, copy in zip((2, 3, 0, 1), ret_copies):
        @pl.when(send_wraps(i))
        def _(i=i, copy=copy):
            copy.wait_recv()
            for j in range(NBLK):
                own[j] = own[j] + (returned(i, 0, j) + returned(i, 1, j))
    for j in range(NBLK):
        xx[j * BLK : (j + 1) * BLK, : 2 * HD] = own[j].astype(BF16)

    for k in range(g.T):
        rows = slice(k * g.SLAB, (k + 1) * g.SLAB)
        ts[k] = nt(wall[rows, :], xx[...]).astype(BF16)
    t_copies = []
    for k in range(1, g.T):
        t_copies.append(
            remote(ts.at[t_index(k)], tr.at[k - 1], t_ss.at[k - 1], t_rs.at[k - 1], t_peer(k))
        )
    dots = jnp.zeros((1, ROWS), F32)
    for k in range(g.T):
        rows = slice(k * g.SLAB, (k + 1) * g.SLAB)
        dots = dots + jnp.sum(ts[k].astype(F32) * x_t[rows, :].astype(F32), axis=0, keepdims=True)
    rd_s[...] = dots
    d_copies = []
    for k in range(1, g.T):
        d_copies.append(remote(rd_s, rd_r.at[k - 1], d_ss.at[k - 1], d_rs.at[k - 1], t_peer(k)))

    ga1 = gather_a(b1, bb1, aga1, ga1_ss, ga1_rs)

    total = us[tn].astype(F32)
    for k, copy in enumerate(u_copies):
        copy.wait_recv()
        total = total + ur[k].astype(F32)
    upd_ref[...] = total.astype(BF16)

    total = ts[tn].astype(F32)
    for k, copy in enumerate(t_copies):
        copy.wait_recv()
        total = total + tr[k].astype(F32)
    for k, copy in enumerate(d_copies):
        copy.wait_recv()
        dots = dots + rd_r[k]
    inv_lane = inv_row[...]
    slab = x_t[pl.ds(pl.multiple_of(tn * g.SLAB, g.SLAB), g.SLAB), :].astype(F32) * inv_lane
    row_mean = dots * inv_lane * (1.0 / D)
    br_ref[...] = (inv_lane * (total - slab * row_mean)).astype(BF16)

    ga2 = gather_a(b2, bb2, aga2, ga2_ss, ga2_rs)

    for copy in ga1:
        copy.wait_recv()
    for a in range(g.NA):
        r, c = a // lane_blocks, a % lane_blocks
        w_ref[0, r * g.CR : (r + 1) * g.CR, c * BLK : (c + 1) * BLK] = aga1[a].astype(F32) * g.factor
    for copy in ga2:
        copy.wait_recv()
    for a in range(g.NA):
        r, c = a // lane_blocks, a % lane_blocks
        w_ref[1, r * g.CR : (r + 1) * g.CR, c * BLK : (c + 1) * BLK] = aga2[a].astype(F32) * g.factor

    started += kv_copies + ret_copies + u_copies + t_copies + d_copies
    started += b2 + ga1 + ga2
    for copy in started:
        copy.wait_send()
    for i in range(4):
        @pl.when(send_wraps(i))
        def _(i=i):
            row_copy(i).wait_send()

        @pl.when(recv_wraps(i))
        def _(i=i):
            pass_copy(i).wait_send()


def write_kernel(upd, br, w, o0, o1, o2, o3, o4, o5, sems):
    pairs = [
        (upd, o0), (br, o1),
        (w.at[0, 0:HD], o2), (w.at[1, 0:HD], o3), (w.at[1, HD : 2 * HD], o4), (w.at[0, HD : 2 * HD], o5),
    ]
    copies = [pltpu.make_async_copy(src, dst, sems.at[i]) for i, (src, dst) in enumerate(pairs)]
    for copy in copies:
        copy.start()
    for copy in copies:
        copy.wait()


def write_out(g, upd, br, w):
    slab = jax.ShapeDtypeStruct((g.SLAB, ROWS), BF16)
    grad = jax.ShapeDtypeStruct((HD, D), F32)
    return pl.pallas_call(
        write_kernel,
        out_shape=[slab, slab, grad, grad, grad, grad],
        in_specs=[pl.BlockSpec(memory_space=pl.ANY)] * 3,
        out_specs=[pl.BlockSpec(memory_space=pltpu.HBM)] * 6,
        scratch_shapes=[pltpu.SemaphoreType.DMA((6,))],
        compiler_params=pltpu.CompilerParams(vmem_limit_bytes=4 * 1024 * 1024),
        name="write",
    )(upd, br, w)


def body(g, states, w_query, w_key, w_value, w_out, send_blocks, neighbor_blocks, cotangent):
    vmem = pl.BlockSpec(memory_space=pltpu.VMEM)
    sem = pltpu.SemaphoreType.DMA
    blocks = (BLK, 2 * HD)
    reduce_bufs = [
        pltpu.VMEM((g.NA, g.CR, 128), BF16),
        pltpu.VMEM((max(g.NA - 1, 1), g.CR, 128), BF16),
        pltpu.VMEM((g.NB, g.CR, 128), BF16),
        pltpu.VMEM((g.NA, g.CR, 128), BF16),
    ]
    na, nbb, nt_ = max(g.NA - 1, 1), max(g.NB - 1, 1), max(g.T - 1, 1)
    reduce_sems = [sem((n,)) for n in (na, na, nbb, nbb, na, na)]
    inputs = (
        jnp.swapaxes(send_blocks, 1, 2), neighbor_blocks, states[0],
        w_query.T, w_key.T, w_value.T, w_out, cotangent[0],
    )
    out = pl.pallas_call(
        functools.partial(kernel, g),
        out_shape=[
            jax.ShapeDtypeStruct((g.SLAB, ROWS), BF16),
            jax.ShapeDtypeStruct((g.SLAB, ROWS), BF16),
            jax.ShapeDtypeStruct((2, 2 * HD, D), F32),
        ],
        in_specs=[pl.BlockSpec(memory_space=pltpu.HBM)] * 8,
        out_specs=[vmem] * 3,
        scratch_shapes=[
            pltpu.SMEM((1, 2, 4), jnp.int32),
            pltpu.SMEM((NBLK, 3), jnp.int32),
            pltpu.VMEM((ROWS, D), BF16),
            pltpu.VMEM((ROWS, D), BF16),
            sem((8,)),
            pltpu.VMEM((NBLK, BLK, D), BF16),
            pltpu.VMEM((D, ROWS), BF16),
            pltpu.VMEM((4 * HD, D), BF16),
            pltpu.VMEM((D, 4 * HD), BF16),
            pltpu.VMEM((D, HD), BF16),
            pltpu.VMEM((2 * HD, D), BF16),
            pltpu.VMEM((1, ROWS), F32),
            pltpu.VMEM((NBLK, 2 * BLK, 2 * HD), BF16),
            pltpu.VMEM((NBLK,) + blocks, BF16),
            pltpu.VMEM((3 * NBLK,) + blocks, BF16),
            pltpu.VMEM((3 * NBLK,) + blocks, BF16),
            pltpu.VMEM((4, 2) + blocks, BF16),
            pltpu.VMEM((4 * NBLK,) + blocks, F32),
            pltpu.VMEM((HD, ROWS), BF16),
            pltpu.VMEM((HD, ROWS), BF16),
            pltpu.VMEM((ROWS, 4 * HD), BF16),
            pltpu.VMEM((NBLK,) + blocks, F32),
            pltpu.VMEM((4, 2) + blocks, BF16),
            pltpu.VMEM((4, 2) + blocks, BF16),
            pltpu.VMEM((g.T, g.SLAB, ROWS), BF16),
            pltpu.VMEM((nt_, g.SLAB, ROWS), BF16),
            pltpu.VMEM((g.T, g.SLAB, ROWS), BF16),
            pltpu.VMEM((nt_, g.SLAB, ROWS), BF16),
            pltpu.VMEM((1, ROWS), F32),
            pltpu.VMEM((nt_, 1, ROWS), F32),
            pltpu.VMEM((2 * HD, ROWS), BF16),
            pltpu.VMEM((4, BLK, D), BF16),
            pltpu.VMEM((4, 2, BLK, D), BF16),
            pltpu.VMEM((2 * HD, D), F32),
        ]
        + reduce_bufs
        + reduce_bufs
        + [sem((4,))] * 8
        + [sem((nt_,))] * 6
        + reduce_sems
        + reduce_sems,
        compiler_params=pltpu.CompilerParams(
            collective_id=0, has_side_effects=True, vmem_limit_bytes=40 * 1024 * 1024
        ),
        name="layer",
    )(
        *[pltpu.with_memory_space_constraint(value, pltpu.HBM) for value in inputs]
    )
    done = write_out(g, *out)
    return (done[0].T[None], done[1].T[None], done[2].T, done[3].T, done[4].T, done[5])


def solution(mesh):
    placed = (
        P("dp", "dom", None),
        P(None, "tensor"),
        P(None, "tensor"),
        P(None, "tensor"),
        P("tensor", None),
        P("dom", None, None),
        P("dom", None),
        P("dp", "dom", None),
    )
    g = Sizes(mesh.shape["dp"], mesh.shape["dom"], mesh.shape["tensor"])
    return jax.shard_map(
        functools.partial(body, g),
        mesh=mesh,
        in_specs=placed,
        out_specs=(
            P("dp", "dom", "tensor"),
            P("dp", "dom", "tensor"),
            P(None, "tensor"),
            P(None, "tensor"),
            P(None, "tensor"),
            P("tensor", None),
        ),
        check_vma=False,
    )
```

```python
import functools
import math

import jax
import jax.numpy as jnp
from jax import lax
from jax.experimental import pallas as pl
from jax.experimental.pallas import tpu as pltpu
from jax.sharding import PartitionSpec as P

BLK = 128
HD = 64
D = 512
NBLK = 4
ROWS = NBLK * BLK
OFFSETS = (1, -1, 2, -2)
NY = 4
F32 = jnp.float32
BF16 = jnp.bfloat16
MESH = pl.DeviceIdType.MESH
EXP_SCALE = (1.0 / math.sqrt(HD)) / math.log(2.0)
SHRINK = 1.0 / math.sqrt(HD)


def nn(a, b):
    return lax.dot_general(a, b, (((1,), (0,)), ((), ())), preferred_element_type=F32)


def nt(a, b):
    return lax.dot_general(a, b, (((1,), (1,)), ((), ())), preferred_element_type=F32)


class Sizes:
    def __init__(self, dp, dom, t):
        self.DP, self.DOM, self.T = dp, dom, t
        nz = dom // NY
        self.ZR = min(4, nz)
        self.ZQ = nz // self.ZR
        self.NA = NY * self.ZR
        self.NB = self.ZQ * dp
        self.CR = 512 // self.NA
        self.SLAB = D // t
        self.factor = 1.0 / math.sqrt(dp * dom * ROWS)


def kernel(
    g,
    sb_any, nb_any, x_any, wq_any, wk_any, wv_any, wo_any, cot_any,
    upd_ref, br_ref, w_ref,
    sb, nb, x_ref, cot_ref, in_sems, unit_b, x_t, wall_t, wall, wo_t, wo_pad, inv_row, bm, kv_own, pool, pool_t, kvs,
    cg, mix_t, qg_t, xx, own, ret_s, ret_r,
    us, ur, ts, tr, rd_s, rd_r, kvg_t, rows_s, rows_r, gkv,
    pay1, rsa1, bb1, aga1, pay2, rsa2, bb2, aga2,
    kv_ss, kv_rs, ret_ss, ret_rs, row_ss, row_rs, pass_ss, pass_rs, u_ss, u_rs, t_ss, t_rs, d_ss, d_rs,
    a1_ss, a1_rs, b1_ss, b1_rs, ga1_ss, ga1_rs,
    a2_ss, a2_rs, b2_ss, b2_rs, ga2_ss, ga2_rs,
):
    dp = lax.axis_index("dp")
    dom = lax.axis_index("dom")
    tn = lax.axis_index("tensor")
    y = lax.rem(dom, NY)
    z = dom // NY
    zr = lax.rem(z, g.ZR)
    zq = z // g.ZR
    my_a = y * g.ZR + zr
    my_b = dp * g.ZQ + zq

    def dom_peer(o):
        return (dp, lax.rem(dom + (o + g.DOM), g.DOM), tn)

    def t_index(k):
        return lax.rem(tn + k, g.T)

    def t_peer(k):
        return (dp, dom, t_index(k))

    a_offs = [(dy, dz) for dy in range(NY) for dz in range(g.ZR)][1:]
    b_offs = [(dd, dq) for dd in range(g.DP) for dq in range(g.ZQ)][1:]

    def a_peer(off):
        y2 = lax.rem(y + off[0], NY)
        r2 = lax.rem(zr + off[1], g.ZR)
        return y2 * g.ZR + r2, (dp, (zq * g.ZR + r2) * NY + y2, tn)

    def b_peer(off):
        d2 = lax.rem(dp + off[0], g.DP)
        q2 = lax.rem(zq + off[1], g.ZQ)
        return d2 * g.ZQ + q2, (d2, (q2 * g.ZR + zr) * NY + y, tn)

    def far(size, d):
        return min(d, size - d)

    b_offs.sort(key=lambda off: -(16 * off[0] + 4 * off[1] if not off[0] else 16 - 4 * off[1]))
    a_offs.sort(key=lambda off: -(far(NY, off[0]) + (3 if off[1] else 0)))
    peers = [dom_peer(o) for o in OFFSETS]
    peers += [t_peer(k) for k in range(1, g.T)]
    peers += [a_peer(off)[1] for off in a_offs]
    peers += [b_peer(off)[1] for off in b_offs]
    barrier = pltpu.get_barrier_semaphore()
    for peer in peers:
        pl.semaphore_signal(barrier, inc=1, device_id=peer, device_id_type=MESH)

    fetches = [
        pltpu.make_async_copy(src, dst, in_sems.at[i])
        for i, (src, dst) in enumerate(
            (
                (x_any, x_ref),
                (wk_any, wall_t.at[0:HD]),
                (wv_any, wall_t.at[HD : 2 * HD]),
                (wq_any, wall_t.at[2 * HD : 3 * HD]),
                (wo_any, wo_pad.at[HD : 2 * HD]),
                (cot_any, cot_ref),
                (sb_any, sb),
                (nb_any, nb),
            )
        )
    ]
    for copy in fetches:
        copy.start()
    def remote(src, dst, ss, rs, peer):
        copy = pltpu.make_async_remote_copy(
            src_ref=src, dst_ref=dst, send_sem=ss, recv_sem=rs, device_id=peer, device_id_type=MESH
        )
        copy.start()
        return copy

    started = []

    fetches[0].wait()
    fetches[1].wait()
    fetches[2].wait()
    for b in range(NBLK):
        rows = slice(b * BLK, (b + 1) * BLK)
        xf = x_ref[rows, :].astype(F32)
        inv = lax.rsqrt(jnp.mean(xf * xf, axis=-1, keepdims=True) + 1e-05)
        unit_b[b] = (xf * inv).astype(BF16)
    for b in range(NBLK):
        rows = slice(b * BLK, (b + 1) * BLK)
        block = nt(unit_b[b], wall_t[: 2 * HD, :]).astype(BF16)
        kv_own[b] = block
        pool[b] = block
    fetches[6].wait()
    fetches[7].wait()
    for i in range(4):
        for c in range(2):
            kvs[i, c] = kv_own[sb[0, c, i]]
    pl.semaphore_wait(barrier, len(peers))
    kv_copies = []
    for i in (2, 3, 0, 1):
        kv_copies.append(
            remote(kvs.at[i], pool.at[pl.ds(NBLK + 2 * i, 2)], kv_ss.at[i], kv_rs.at[i], dom_peer(OFFSETS[i]))
        )

    half = lax.rem(tn, 2)

    def late(part):
        return jnp.logical_or(part < 2, part >= g.DOM - 2)

    def send_wraps(i):
        return late(lax.rem(dom + (OFFSETS[i] + g.DOM), g.DOM))

    def recv_wraps(i):
        return late(dom)

    def row_copy(i):
        return pltpu.make_async_remote_copy(
            src_ref=rows_s.at[i], dst_ref=rows_r.at[i, half], send_sem=row_ss.at[i], recv_sem=row_rs.at[i],
            device_id=dom_peer(OFFSETS[i]), device_id_type=MESH,
        )

    def pass_copy(i):
        return pltpu.make_async_remote_copy(
            src_ref=rows_r.at[i, half], dst_ref=rows_r.at[i, half], send_sem=pass_ss.at[i], recv_sem=pass_rs.at[i],
            device_id=(dp, dom, tn + 1 - 2 * half), device_id_type=MESH,
        )

    for i in (2, 3, 0, 1):
        @pl.when(send_wraps(i))
        def _(i=i):
            rows_s[i] = unit_b[sb[0, half, i]]
            row_copy(i).start()

    wo_pad[0:HD, :] = jnp.zeros((HD, D), BF16)
    wall_t[3 * HD :, :] = jnp.zeros((HD, D), BF16)
    fetches[3].wait()
    fetches[4].wait()
    fetches[5].wait()
    for b in range(NBLK):
        rows = slice(b * BLK, (b + 1) * BLK)
        bm[b, 0:BLK, :] = nt(unit_b[b], wall_t[2 * HD :, :]).astype(BF16)
        bm[b, BLK : 2 * BLK, :] = nt(cot_ref[rows, :], wo_pad[...]).astype(BF16)
        pool_t[b] = kv_own[b].T
    for f in range(D // BLK):
        cols = slice(f * BLK, (f + 1) * BLK)
        for b in range(NBLK):
            x_t[cols, b * BLK : (b + 1) * BLK] = x_ref[b * BLK : (b + 1) * BLK, cols].T
        wo_t[cols, :] = wo_pad[HD : 2 * HD, cols].T
        wall[cols, :] = wall_t[:, cols].T
    square = jnp.zeros((1, ROWS), F32)
    for f in range(D // BLK):
        part = x_t[f * BLK : (f + 1) * BLK, :].astype(F32)
        square = square + jnp.sum(part * part, axis=0, keepdims=True)
    inv_lane = lax.rsqrt(square * (1.0 / D) + 1e-05)
    inv_row[...] = inv_lane

    for copy in kv_copies:
        copy.wait_recv()
    for p in range(NBLK, 3 * NBLK):
        pool_t[p] = pool[p].T

    for b in range(NBLK):
        lists = [nb[b, n] for n in range(3)]
        kv_sel = jnp.concatenate([pool[b]] + [pool[i] for i in lists], axis=0)
        kv_sel_t = jnp.concatenate([pool_t[b]] + [pool_t[i] for i in lists], axis=1)
        both = nt(kv_sel, bm[b])
        scores = both[:, :BLK]
        prob_grad = both[:, BLK:]
        powers = jnp.exp2((scores - jnp.max(scores, axis=0, keepdims=True)) * EXP_SCALE)
        weights = powers * (1.0 / jnp.sum(powers, axis=0, keepdims=True))
        inner = jnp.sum(weights * prob_grad, axis=0, keepdims=True)
        score_low = (weights * (prob_grad - inner) * SHRINK).astype(BF16)
        pair = jnp.concatenate([score_low, weights.astype(BF16)], axis=1)
        grads = nn(pair, bm[b])
        for n in range(4):
            cg[4 * b + n] = grads[n * BLK : (n + 1) * BLK, :]
        outs = nn(kv_sel_t, pair)
        cols = slice(b * BLK, (b + 1) * BLK)
        qg_t[:, cols] = outs[0:HD, 0:BLK].astype(BF16)
        mix_t[:, cols] = outs[HD : 2 * HD, BLK : 2 * BLK].astype(BF16)

    def listed_sum(p, start):
        total = start
        for b in range(NBLK):
            for n in range(3):
                term = jnp.where(nb[b, n] == p, cg[4 * b + n + 1], 0.0)
                total = term if total is None else total + term
        return total

    ret_copies = []
    for i in (2, 3, 0, 1):
        for c in range(2):
            ret_s[i, c] = listed_sum(NBLK + 2 * i + c, None).astype(BF16)
        ret_copies.append(
            remote(ret_s.at[i], ret_r.at[i], ret_ss.at[i], ret_rs.at[i], dom_peer(-OFFSETS[i]))
        )

    for k in range(g.T):
        us[k] = nn(wo_t[k * g.SLAB : (k + 1) * g.SLAB, :], mix_t[...]).astype(BF16)
    u_copies = []
    for k in range(1, g.T):
        u_copies.append(
            remote(us.at[t_index(k)], ur.at[k - 1], u_ss.at[k - 1], u_rs.at[k - 1], t_peer(k))
        )

    def scatter_a(pay, rsa, ss, rs):
        copies = []
        for k, off in enumerate(a_offs):
            index, peer = a_peer(off)
            copies.append(remote(pay.at[index], rsa.at[k], ss.at[k], rs.at[k], peer))
        return copies

    def spread_b(copies, pay, rsa, bb, ss, rs):
        total = pay[my_a].astype(F32)
        for k, copy in enumerate(copies):
            copy.wait_recv()
            total = total + rsa[k].astype(F32)
        bb[my_b] = total.astype(BF16)
        copies = []
        for k, off in enumerate(b_offs):
            copies.append(remote(bb.at[my_b], bb.at[my_b], ss.at[k], rs.at[k], b_peer(off)[1]))
        return copies

    def gather_a(copies, bb, aga, ss, rs):
        for copy in copies:
            copy.wait_recv()
        total = bb[0].astype(F32)
        for j in range(1, g.NB):
            total = total + bb[j].astype(F32)
        aga[my_a] = total.astype(BF16)
        copies = []
        for k, off in enumerate(a_offs):
            copies.append(remote(aga.at[my_a], aga.at[my_a], ss.at[k], rs.at[k], a_peer(off)[1]))
        return copies

    unit = unit_b[...].reshape(ROWS, D)
    grad_q = nn(qg_t[...], unit)
    grad_o = nn(mix_t[...], cot_ref[...])
    lane_blocks = D // BLK
    for a in range(g.NA):
        r, c = a // lane_blocks, a % lane_blocks
        row = r * g.CR
        cols = slice(c * BLK, (c + 1) * BLK)
        if row < HD:
            pay1[a] = grad_q[row : row + g.CR, cols].astype(BF16)
        else:
            pay1[a] = grad_o[row - HD : row - HD + g.CR, cols].astype(BF16)
    a1 = scatter_a(pay1, rsa1, a1_ss, a1_rs)
    started += a1

    for j in range(NBLK):
        own[j] = listed_sum(j, cg[4 * j])
    for b in range(NBLK):
        rows = slice(b * BLK, (b + 1) * BLK)
        query_grad = qg_t[:, rows].astype(F32).T.astype(BF16)
        xx[rows, 2 * HD :] = jnp.concatenate([query_grad, jnp.zeros((BLK, HD), BF16)], axis=1)


    for i in (2, 3, 0, 1):
        @pl.when(recv_wraps(i))
        def _(i=i):
            row_copy(i).wait_recv()
            pass_copy(i).start()

    def returned(i, c, j):
        return jnp.where(sb[0, c, i] == j, ret_r[i, c].astype(F32), 0.0)

    for i, copy in zip((2, 3, 0, 1), ret_copies):
        @pl.when(jnp.logical_not(send_wraps(i)))
        def _(i=i, copy=copy):
            copy.wait_recv()
            for j in range(NBLK):
                own[j] = own[j] + (returned(i, 0, j) + returned(i, 1, j))
    for j in range(NBLK):
        kvg_t[:, j * BLK : (j + 1) * BLK] = own[j].astype(BF16).T
    gkv[...] = nn(kvg_t[...], unit)
    for i in (2, 3, 0, 1):
        @pl.when(recv_wraps(i))
        def _(i=i):
            pass_copy(i).wait_recv()
            for c in range(2):
                gkv[...] += nn(ret_s[i, c].T, rows_r[i, c])
    for a in range(g.NA):
        r, c = a // lane_blocks, a % lane_blocks
        pay2[a] = gkv[r * g.CR : (r + 1) * g.CR, c * BLK : (c + 1) * BLK].astype(BF16)
    a2 = scatter_a(pay2, rsa2, a2_ss, a2_rs)
    started += a2
    b2 = spread_b(a2, pay2, rsa2, bb2, b2_ss, b2_rs)
    b1 = spread_b(a1, pay1, rsa1, bb1, b1_ss, b1_rs)
    started += b1

    for i, copy in zip((2, 3, 0, 1), ret_copies):
        @pl.when(send_wraps(i))
        def _(i=i, copy=copy):
            copy.wait_recv()
            for j in range(NBLK):
                own[j] = own[j] + (returned(i, 0, j) + returned(i, 1, j))
    for j in range(NBLK):
        xx[j * BLK : (j + 1) * BLK, : 2 * HD] = own[j].astype(BF16)

    for k in range(g.T):
        rows = slice(k * g.SLAB, (k + 1) * g.SLAB)
        ts[k] = nt(wall[rows, :], xx[...]).astype(BF16)
    t_copies = []
    for k in range(1, g.T):
        t_copies.append(
            remote(ts.at[t_index(k)], tr.at[k - 1], t_ss.at[k - 1], t_rs.at[k - 1], t_peer(k))
        )
    dots = jnp.zeros((1, ROWS), F32)
    for k in range(g.T):
        rows = slice(k * g.SLAB, (k + 1) * g.SLAB)
        dots = dots + jnp.sum(ts[k].astype(F32) * x_t[rows, :].astype(F32), axis=0, keepdims=True)
    rd_s[...] = dots
    d_copies = []
    for k in range(1, g.T):
        d_copies.append(remote(rd_s, rd_r.at[k - 1], d_ss.at[k - 1], d_rs.at[k - 1], t_peer(k)))


    ga2 = gather_a(b2, bb2, aga2, ga2_ss, ga2_rs)
    ga1 = gather_a(b1, bb1, aga1, ga1_ss, ga1_rs)

    total = us[tn].astype(F32)
    for k, copy in enumerate(u_copies):
        copy.wait_recv()
        total = total + ur[k].astype(F32)
    upd_ref[...] = total.astype(BF16)

    total = ts[tn].astype(F32)
    for k, copy in enumerate(t_copies):
        copy.wait_recv()
        total = total + tr[k].astype(F32)
    for k, copy in enumerate(d_copies):
        copy.wait_recv()
        dots = dots + rd_r[k]
    inv_lane = inv_row[...]
    slab = x_t[pl.ds(pl.multiple_of(tn * g.SLAB, g.SLAB), g.SLAB), :].astype(F32) * inv_lane
    row_mean = dots * inv_lane * (1.0 / D)
    br_ref[...] = (inv_lane * (total - slab * row_mean)).astype(BF16)


    for copy in ga1:
        copy.wait_recv()
    for a in range(g.NA):
        r, c = a // lane_blocks, a % lane_blocks
        w_ref[0, r * g.CR : (r + 1) * g.CR, c * BLK : (c + 1) * BLK] = aga1[a].astype(F32) * g.factor
    for copy in ga2:
        copy.wait_recv()
    for a in range(g.NA):
        r, c = a // lane_blocks, a % lane_blocks
        w_ref[1, r * g.CR : (r + 1) * g.CR, c * BLK : (c + 1) * BLK] = aga2[a].astype(F32) * g.factor

    started += kv_copies + ret_copies + u_copies + t_copies + d_copies
    started += b2 + ga1 + ga2
    for copy in started:
        copy.wait_send()
    for i in range(4):
        @pl.when(send_wraps(i))
        def _(i=i):
            row_copy(i).wait_send()

        @pl.when(recv_wraps(i))
        def _(i=i):
            pass_copy(i).wait_send()


def write_kernel(upd, br, w, o0, o1, o2, o3, o4, o5, sems):
    pairs = [
        (upd, o0), (br, o1),
        (w.at[0, 0:HD], o2), (w.at[1, 0:HD], o3), (w.at[1, HD : 2 * HD], o4), (w.at[0, HD : 2 * HD], o5),
    ]
    copies = [pltpu.make_async_copy(src, dst, sems.at[i]) for i, (src, dst) in enumerate(pairs)]
    for copy in copies:
        copy.start()
    for copy in copies:
        copy.wait()


def write_out(g, upd, br, w):
    slab = jax.ShapeDtypeStruct((g.SLAB, ROWS), BF16)
    grad = jax.ShapeDtypeStruct((HD, D), F32)
    return pl.pallas_call(
        write_kernel,
        out_shape=[slab, slab, grad, grad, grad, grad],
        in_specs=[pl.BlockSpec(memory_space=pl.ANY)] * 3,
        out_specs=[pl.BlockSpec(memory_space=pltpu.HBM)] * 6,
        scratch_shapes=[pltpu.SemaphoreType.DMA((6,))],
        compiler_params=pltpu.CompilerParams(vmem_limit_bytes=4 * 1024 * 1024),
        name="write",
    )(upd, br, w)


def body(g, states, w_query, w_key, w_value, w_out, send_blocks, neighbor_blocks, cotangent):
    vmem = pl.BlockSpec(memory_space=pltpu.VMEM)
    sem = pltpu.SemaphoreType.DMA
    blocks = (BLK, 2 * HD)
    reduce_bufs = [
        pltpu.VMEM((g.NA, g.CR, 128), BF16),
        pltpu.VMEM((max(g.NA - 1, 1), g.CR, 128), BF16),
        pltpu.VMEM((g.NB, g.CR, 128), BF16),
        pltpu.VMEM((g.NA, g.CR, 128), BF16),
    ]
    na, nbb, nt_ = max(g.NA - 1, 1), max(g.NB - 1, 1), max(g.T - 1, 1)
    reduce_sems = [sem((n,)) for n in (na, na, nbb, nbb, na, na)]
    inputs = (
        jnp.swapaxes(send_blocks, 1, 2), neighbor_blocks, states[0],
        w_query.T, w_key.T, w_value.T, w_out, cotangent[0],
    )
    out = pl.pallas_call(
        functools.partial(kernel, g),
        out_shape=[
            jax.ShapeDtypeStruct((g.SLAB, ROWS), BF16),
            jax.ShapeDtypeStruct((g.SLAB, ROWS), BF16),
            jax.ShapeDtypeStruct((2, 2 * HD, D), F32),
        ],
        in_specs=[pl.BlockSpec(memory_space=pltpu.HBM)] * 8,
        out_specs=[vmem] * 3,
        scratch_shapes=[
            pltpu.SMEM((1, 2, 4), jnp.int32),
            pltpu.SMEM((NBLK, 3), jnp.int32),
            pltpu.VMEM((ROWS, D), BF16),
            pltpu.VMEM((ROWS, D), BF16),
            sem((8,)),
            pltpu.VMEM((NBLK, BLK, D), BF16),
            pltpu.VMEM((D, ROWS), BF16),
            pltpu.VMEM((4 * HD, D), BF16),
            pltpu.VMEM((D, 4 * HD), BF16),
            pltpu.VMEM((D, HD), BF16),
            pltpu.VMEM((2 * HD, D), BF16),
            pltpu.VMEM((1, ROWS), F32),
            pltpu.VMEM((NBLK, 2 * BLK, 2 * HD), BF16),
            pltpu.VMEM((NBLK,) + blocks, BF16),
            pltpu.VMEM((3 * NBLK,) + blocks, BF16),
            pltpu.VMEM((3 * NBLK,) + blocks, BF16),
            pltpu.VMEM((4, 2) + blocks, BF16),
            pltpu.VMEM((4 * NBLK,) + blocks, F32),
            pltpu.VMEM((HD, ROWS), BF16),
            pltpu.VMEM((HD, ROWS), BF16),
            pltpu.VMEM((ROWS, 4 * HD), BF16),
            pltpu.VMEM((NBLK,) + blocks, F32),
            pltpu.VMEM((4, 2) + blocks, BF16),
            pltpu.VMEM((4, 2) + blocks, BF16),
            pltpu.VMEM((g.T, g.SLAB, ROWS), BF16),
            pltpu.VMEM((nt_, g.SLAB, ROWS), BF16),
            pltpu.VMEM((g.T, g.SLAB, ROWS), BF16),
            pltpu.VMEM((nt_, g.SLAB, ROWS), BF16),
            pltpu.VMEM((1, ROWS), F32),
            pltpu.VMEM((nt_, 1, ROWS), F32),
            pltpu.VMEM((2 * HD, ROWS), BF16),
            pltpu.VMEM((4, BLK, D), BF16),
            pltpu.VMEM((4, 2, BLK, D), BF16),
            pltpu.VMEM((2 * HD, D), F32),
        ]
        + reduce_bufs
        + reduce_bufs
        + [sem((4,))] * 8
        + [sem((nt_,))] * 6
        + reduce_sems
        + reduce_sems,
        compiler_params=pltpu.CompilerParams(
            collective_id=0, has_side_effects=True, vmem_limit_bytes=40 * 1024 * 1024
        ),
        name="layer",
    )(
        *[pltpu.with_memory_space_constraint(value, pltpu.HBM) for value in inputs]
    )
    done = write_out(g, *out)
    return (done[0].T[None], done[1].T[None], done[2].T, done[3].T, done[4].T, done[5])


def solution(mesh):
    placed = (
        P("dp", "dom", None),
        P(None, "tensor"),
        P(None, "tensor"),
        P(None, "tensor"),
        P("tensor", None),
        P("dom", None, None),
        P("dom", None),
        P("dp", "dom", None),
    )
    g = Sizes(mesh.shape["dp"], mesh.shape["dom"], mesh.shape["tensor"])
    return jax.shard_map(
        functools.partial(body, g),
        mesh=mesh,
        in_specs=placed,
        out_specs=(
            P("dp", "dom", "tensor"),
            P("dp", "dom", "tensor"),
            P(None, "tensor"),
            P(None, "tensor"),
            P(None, "tensor"),
            P("tensor", None),
        ),
        check_vma=False,
    )
```
